768 devices in a mesh: down: 192 (over y, z, core), cross: 4 (over x).
Axes of the slice: x: 4, y: 8, z: 12, core: 2. Of those that a mesh axis runs over, the one named last changes fastest.
Arguments:
- right_side: float32 [1536, 128, 256], P('down', 'cross'), may hold values from -6 to 6
- kappa: float32 [1536, 128, 256], P('down', 'cross'), may hold values from 0.3 to 3
- band_mask: int32 [1536, 128, 256], P('down', 'cross'), may hold values 0 or 1
- tile_route: int32 [192, 16], P('down', 'cross'), may hold values from -1 to 7, as said below
Outputs:
- pressure: float32 [1536, 128, 256], P('down', 'cross')
The draws below stay inside these ranges and needn't reach their ends.
Inputs may be any that keep to these rules, and one draw needn't show every extreme that they name: `tile_route`: within the tiles of one device each value other than -1 occurs at most once; in every draw some owner receives 2 tiles from every device of its cross-slope group.
All inputs are finite; a program needn't handle non-finite values. No bound on the sum of `band_mask` on one device may be relied on, other than what follows from the above.
Results may differ from the reference program's by a relative error of at most 0.0003.
Values sent between devices are 32-bit elements; how exact they have to be, the bound alone decides.
A program may use at most 64 MiB of HBM per device.

```python
import math
import jax
import jax.numpy as jnp
from jax import lax

CX = 8
CY = 32
NZ = 256
TPD = 4
SLOTS = 2
BLOCK_SWEEPS = 4
COARSE_ITERS = 12
NX = 1536
NY = 128
N_DOWN = 192
N_CROSS = 4


def draw_tile_route(key, part):
    key_cloud = jax.random.fold_in(key, 11)
    key_row = jax.random.fold_in(key, 12)
    key_base = jax.random.fold_in(key, 13)
    cloud = (jax.random.randint(key_cloud, (N_DOWN, N_CROSS, TPD), 0, 8) > 0).astype(jnp.int32)
    chosen = jax.random.randint(key_row, (), 0, N_DOWN)
    row_ids = jnp.arange(N_DOWN)[:, None, None]
    cloud = jnp.where(row_ids == chosen, 1, cloud)
    base = jax.random.randint(key_base, (N_DOWN, 1, 1), 0, N_CROSS)
    base = jnp.where(row_ids == chosen, N_CROSS - 2, base)
    ranks = jnp.cumsum(cloud, axis=2) - cloud
    owner = (base + ranks // SLOTS) % N_CROSS
    value = owner * SLOTS + ranks % SLOTS
    route = jnp.where(cloud == 1, value, -1)
    return route.reshape(N_DOWN, N_CROSS * TPD).astype(jnp.int32)


def with_ends(array, own_key, least, largest):
    longest = array.shape.index(max(array.shape))
    spots = []
    for shift in (0, 1):
        where = [jax.random.randint(jax.random.fold_in(own_key, axis), (), 0, length) for axis, length in enumerate(array.shape)]
        where[longest] = (where[longest] + shift) % array.shape[longest]
        spots.append(tuple(where))
    return array.at[spots[0]].set(least).at[spots[1]].set(largest)


def levels(own_key, shape, cuts, low, top_value):
    def one(axis_at, parts):
        draws = jax.random.uniform(jax.random.fold_in(jax.random.fold_in(own_key, 6), axis_at), (parts,), jnp.float32, low / len(cuts), top_value / len(cuts))
        return jnp.repeat(jnp.exp(draws), shape[axis_at] // parts).reshape((-1,) + (1,) * (len(shape) - axis_at - 1))

    level = one(*cuts[0])
    for cut in cuts[1:]:
        level = level * one(*cut)
    return level


def bell_draw(own_key, shape, scale, reach, pieces=(), held_as=jnp.bfloat16):
    result = jax.random.normal(own_key, shape, jnp.float32) * scale
    if len(pieces) > 0:
        result = levels(own_key, shape, pieces, -0.22, 0.18) * result
    return jnp.clip(result, min=-reach, max=reach).astype(held_as)


def setup_inputs(seed: int = 0) -> dict:
    key_of = jax.random.split(jax.random.key(seed), 5)
    return {
        "right_side": bell_draw(key_of[0], (NX, NY, NZ), 1.0, 6.0, ((0, 192), (1, 4)), jnp.float32),
        "kappa": jnp.clip(jnp.exp(math.log(3.0) - 2.3025851 * jax.random.uniform(key_of[1], (NX, NY, NZ), jnp.float32) ** levels(key_of[1], (NX, NY, NZ), ((0, 192), (1, 4)), -0.2, 0.2)), 0.3, 3.0),
        "band_mask": with_ends((jax.random.randint(key_of[2], (NX, NY, NZ), 0, 3) < 1).astype(jnp.int32), jax.random.fold_in(key_of[2], 1), 0, 1),
        "tile_route": draw_tile_route(jax.random.fold_in(key_of[4], 71), 0),
    }


OMEGA = 0.8
SNOW_FACTOR = 3.0


def pad_all(field):
    return jnp.pad(field, [(0, 0)] * (field.ndim - 3) + [(1, 1)] * 3)


def center(padded):
    return padded[..., 1:-1, 1:-1, 1:-1]


def neighbours(padded):
    return [padded[..., 2:, 1:-1, 1:-1], padded[..., :-2, 1:-1, 1:-1],
            padded[..., 1:-1, 2:, 1:-1], padded[..., 1:-1, :-2, 1:-1],
            padded[..., 1:-1, 1:-1, 2:], padded[..., 1:-1, 1:-1, :-2]]


def stencil(field_pad, conduct_pad, scale):
    middle = center(field_pad)
    kmiddle = center(conduct_pad)
    total = jnp.zeros_like(middle)
    for other, kother in zip(neighbours(field_pad), neighbours(conduct_pad)):
        total = total + scale * (kmiddle + kother) * (middle - other)
    return total


def diagonal(conduct_pad, scale):
    kmiddle = center(conduct_pad)
    total = jnp.zeros_like(kmiddle)
    for kother in neighbours(conduct_pad):
        total = total + scale * (kmiddle + kother)
    return total


def block_smooth(residual, conduct):
    conduct_pad = pad_all(conduct)
    diag = diagonal(conduct_pad, 2.0)
    safe = jnp.where(diag > 0, diag, 1.0)
    fix = OMEGA * residual / safe
    for sweep in range(BLOCK_SWEEPS - 1):
        fix = fix + OMEGA * (residual - stencil(pad_all(fix), conduct_pad, 2.0)) / safe
    return fix


def coarse_solve(totals, link_down, link_cross, outflow):
    link_up = jnp.concatenate([jnp.zeros_like(link_down[:1]), link_down[:-1]], 0)
    link_back = jnp.concatenate([jnp.zeros_like(link_cross[:, :1]), link_cross[:, :-1]], 1)

    def operate(field):
        padded = jnp.pad(field, 1)
        return (outflow * field - link_down * padded[2:, 1:-1] - link_up * padded[:-2, 1:-1]
                - link_cross * padded[1:-1, 2:] - link_back * padded[1:-1, :-2])

    def sweep(step, carry):
        answer, resid, search, norm_now = carry
        image = operate(search)
        alpha = norm_now / jnp.sum(search * image)
        answer = answer + alpha * search
        resid = resid - alpha * image
        norm_next = jnp.sum(resid * resid)
        search = resid + (norm_next / norm_now) * search
        return (answer, resid, search, norm_next)

    start = (jnp.zeros_like(totals), totals, totals, jnp.sum(totals * totals))
    return lax.fori_loop(0, COARSE_ITERS, sweep, start)[0]


def reference(right_side, kappa, band_mask, tile_route):
    conduct = kappa / (1.0 + SNOW_FACTOR * band_mask.astype(jnp.float32))
    conduct_pad = pad_all(conduct)
    diag_fine = diagonal(conduct_pad, 0.5)
    pressure = OMEGA * right_side / diag_fine
    pressure = pressure + OMEGA * (right_side - stencil(pad_all(pressure), conduct_pad, 0.5)) / diag_fine
    residual = right_side - stencil(pad_all(pressure), conduct_pad, 0.5)
    rows_all, cols_all, layers = residual.shape
    half_x, half_y, half_z = CX // 2, CY // 2, layers // 2
    tile_w = half_y // TPD
    coarse_res = residual.reshape(rows_all // 2, 2, cols_all // 2, 2, half_z, 2).sum(axis=(1, 3, 5))
    coarse_con = conduct.reshape(rows_all // 2, 2, cols_all // 2, 2, half_z, 2).sum(axis=(1, 3, 5)) * 0.125
    tiles_res = coarse_res.reshape(N_DOWN, half_x, N_CROSS * TPD, tile_w, half_z).transpose(0, 2, 1, 3, 4)
    tiles_con = coarse_con.reshape(N_DOWN, half_x, N_CROSS * TPD, tile_w, half_z).transpose(0, 2, 1, 3, 4)
    cloud = (tile_route >= 0).astype(jnp.float32)
    tile_fix = block_smooth(tiles_res, tiles_con) * cloud[:, :, None, None, None]
    tile_fix = tile_fix.transpose(0, 2, 1, 3, 4).reshape(rows_all // 2, cols_all // 2, half_z)
    coarse_pad = pad_all(coarse_con)
    faces_down = 2.0 * (coarse_pad[:-1, 1:-1, 1:-1] + coarse_pad[1:, 1:-1, 1:-1])
    link_rows = faces_down[::half_x].sum(axis=2).reshape(N_DOWN + 1, N_CROSS, half_y).sum(axis=2)
    faces_cross = 2.0 * (coarse_pad[1:-1, :-1, 1:-1] + coarse_pad[1:-1, 1:, 1:-1])
    link_cols = faces_cross[:, ::half_y].sum(axis=2).reshape(N_DOWN, half_x, N_CROSS + 1).sum(axis=1)
    vertical = 2.0 * (coarse_con[:, :, 0] + coarse_con[:, :, -1])
    vertical = vertical.reshape(N_DOWN, half_x, N_CROSS, half_y).sum(axis=(1, 3))
    outflow = link_rows[:-1] + link_rows[1:] + link_cols[:, :-1] + link_cols[:, 1:] + vertical
    totals = coarse_res.reshape(N_DOWN, half_x, N_CROSS, half_y, half_z).sum(axis=(1, 3, 4))
    brick_fix = coarse_solve(totals, link_rows[1:], link_cols[:, 1:], outflow)
    spread = jnp.repeat(jnp.repeat(brick_fix, half_x, 0), half_y, 1)
    correction = tile_fix + spread[:, :, None]
    fine_fix = jnp.broadcast_to(correction[:, None, :, None, :, None],
                                (rows_all // 2, 2, cols_all // 2, 2, half_z, 2)).reshape(rows_all, cols_all, layers)
    pressure = pressure + fine_fix
    for sweep in range(2):
        pressure = pressure + OMEGA * (right_side - stencil(pad_all(pressure), conduct_pad, 0.5)) / diag_fine
    return pressure
```

```python
import jax
import jax.numpy as jnp
from jax import lax
from jax.experimental import pallas as pl
from jax.experimental.pallas import tpu as pltpu
from jax.sharding import PartitionSpec as P

OMEGA = 0.8
BLOCK_SWEEPS = 4
COARSE_ITERS = 12
CHIPS_Z = 12

MESH = pl.DeviceIdType.MESH
CORNERS = ((-1, -1), (-1, 1), (1, -1), (1, 1))
F32 = jnp.float32


def iota(shape, dim):
    return lax.broadcasted_iota(jnp.int32, shape, dim)


def flag(cond):
    return jnp.where(cond, 1.0, 0.0).astype(F32)


def total_of(value):
    return jnp.sum(jnp.sum(value, axis=0, keepdims=True), axis=1, keepdims=True)


def side_sum(value):
    rows, lanes = value.shape
    lane = iota(value.shape, 1)
    return (
        pltpu.roll(value, 1, 0)
        + pltpu.roll(value, rows - 1, 0)
        + jnp.where(lane > 0, pltpu.roll(value, 1, 1), 0.0)
        + jnp.where(lane < lanes - 1, pltpu.roll(value, lanes - 1, 1), 0.0)
    )


def tile_side_sum(value):
    rows, lanes = value.shape
    lane = iota(value.shape, 1)
    row = iota(value.shape, 0) % 8
    return (
        jnp.where(row >= 2, pltpu.roll(value, 2, 0), 0.0)
        + jnp.where(row < 6, pltpu.roll(value, rows - 2, 0), 0.0)
        + jnp.where(lane >= 2, pltpu.roll(value, 2, 1), 0.0)
        + jnp.where(lane < lanes - 2, pltpu.roll(value, lanes - 2, 1), 0.0)
    )


def pair_sum(value):
    rows, lanes = value.shape
    row, lane = iota(value.shape, 0), iota(value.shape, 1)
    value = value + jnp.where(row % 2 == 0, pltpu.roll(value, rows - 1, 0), pltpu.roll(value, 1, 0))
    return value + jnp.where(
        lane % 2 == 0, pltpu.roll(value, lanes - 1, 1), pltpu.roll(value, 1, 1)
    )


def make_kernel(n_down, n_cross, nz):
    ny = n_down // (2 * nz)
    half = nz // 2

    def kernel(
        rhs_hbm, kappa_hbm, mask_hbm, route, out,
        E, R, MK, D, W, PA, PB, Q, RES, CR, CC, WT, FA, FB,
        SX, LX, LK, M1, G1, M2, G2, M3, G3,
        load_sem, h_send, h_recv, q_send, q_recv,
        s1, r1, s2, r2, s3, r3,
    ):
        d = lax.axis_index("down")
        c = lax.axis_index("cross")
        core = lax.rem(d, 2)
        chip = lax.div(d, 2)
        z = lax.rem(chip, nz)
        y = lax.div(chip, nz)

        loads = [
            pltpu.make_async_copy(kappa_hbm, E.at[3:11, 8:40, :], load_sem.at[0]),
            pltpu.make_async_copy(mask_hbm, MK, load_sem.at[1]),
            pltpu.make_async_copy(rhs_hbm, R.at[3:11, 8:40, :], load_sem.at[2]),
        ]
        for load in loads:
            load.start()

        d_next, d_prev = lax.rem(d + 1, n_down), lax.rem(d + n_down - 1, n_down)
        c_next, c_prev = lax.rem(c + 1, n_cross), lax.rem(c + n_cross - 1, n_cross)
        near = [(d_prev, c), (d_next, c), (d, c_prev), (d, c_next)]
        corners = [
            (d_prev if sx < 0 else d_next, c_prev if sy < 0 else c_next) for sx, sy in CORNERS
        ]
        n1 = 2 * n_cross
        me1 = c * 2 + core
        group1 = []
        for k in range(1, n1):
            g = lax.rem(me1 + k, n1)
            group1.append((chip * 2 + lax.rem(g, 2), lax.div(g, 2)))
        group2 = [((lax.rem(y + k, ny) * nz + z) * 2 + core, c) for k in range(1, ny)]
        group3 = [((y * nz + lax.rem(z + k, nz)) * 2 + core, c) for k in range(1, nz)]

        barrier = pltpu.get_barrier_semaphore()
        peers = near + corners + group1 + group2 + group3
        for peer in peers:
            pl.semaphore_signal(barrier, inc=1, device_id=peer, device_id_type=MESH)

        m_up, m_dn = flag(d > 0), flag(d < n_down - 1)
        m_l, m_r = flag(c > 0), flag(c < n_cross - 1)

        zero8 = jnp.zeros((8, 256), F32)
        for i in (0, 13):
            E[i, 0:8, :] = zero8
            E[i, 40:48, :] = zero8
        loads[0].wait()
        loads[1].wait()

        @pl.loop(0, 8)
        def _(x):
            kap = E[x + 3, 8:40, :]
            E[x + 3, 8:40, :] = jnp.where(MK[x] > 0, kap * 0.25, kap)

        loads[2].wait()
        sub8 = iota((8, 256), 0)

        @pl.loop(0, 8)
        def _(x):
            SX[0, x] = jnp.where(sub8 < 3, E[x + 3, 8:16, :], pltpu.roll(R[x + 3, 8:16, :], 3, 0))
            SX[1, x] = jnp.where(sub8 >= 5, E[x + 3, 32:40, :], pltpu.roll(R[x + 3, 32:40, :], 5, 0))

        pl.semaphore_wait(barrier, len(peers))

        def remote(src, dst, send, recv, k, peer):
            return pltpu.make_async_remote_copy(
                src_ref=src, dst_ref=dst, send_sem=send.at[k], recv_sem=recv.at[k],
                device_id=peer, device_id_type=MESH,
            )

        halo = [
            remote(E.at[3:6, 8:40, :], E.at[11:14, 8:40, :], h_send, h_recv, 0, near[0]),
            remote(E.at[8:11, 8:40, :], E.at[0:3, 8:40, :], h_send, h_recv, 1, near[1]),
            remote(SX.at[0], LX.at[1], h_send, h_recv, 2, near[2]),
            remote(SX.at[1], LX.at[0], h_send, h_recv, 3, near[3]),
            remote(R.at[3:5, 8:40, :], R.at[11:13, 8:40, :], h_send, h_recv, 4, near[0]),
            remote(R.at[9:11, 8:40, :], R.at[1:3, 8:40, :], h_send, h_recv, 5, near[1]),
        ]
        for k, (sx, sy) in enumerate(CORNERS):
            rows = slice(0, 2) if sx < 0 else slice(6, 8)
            src = SX.at[0 if sy < 0 else 1, rows]
            halo.append(remote(src, LK.at[3 - k], h_send, h_recv, 6 + k, corners[k]))
        for k in (6, 7, 8, 9, 0, 1, 2, 3, 4, 5):
            halo[k].start()
        for copy in halo:
            copy.wait_recv()

        def unpack(tile, i, left, keep):
            if left:
                E[i, 0:8, :] = jnp.where(sub8 >= 5, tile, 0.0) * keep
                R[i, 0:8, :] = jnp.where(sub8 >= 6, pltpu.roll(tile, 3, 0), 0.0) * keep
            else:
                E[i, 40:48, :] = jnp.where(sub8 < 3, tile, 0.0) * keep
                R[i, 40:48, :] = jnp.where(sub8 < 2, pltpu.roll(tile, 5, 0), 0.0) * keep

        @pl.loop(0, 8)
        def _(x):
            unpack(LX[0, x], x + 3, True, m_l)
            unpack(LX[1, x], x + 3, False, m_r)

        @pl.loop(0, 2)
        def _(x):
            unpack(LK[0, x], x + 1, True, m_l * m_up)
            unpack(LK[1, x], x + 1, False, m_r * m_up)
            unpack(LK[2, x], x + 11, True, m_l * m_dn)
            unpack(LK[3, x], x + 11, False, m_r * m_dn)
            R[x + 1, 8:40, :] = R[x + 1, 8:40, :] * m_up
            R[x + 11, 8:40, :] = R[x + 11, 8:40, :] * m_dn

        @pl.loop(0, 3)
        def _(x):
            E[x, 8:40, :] = E[x, 8:40, :] * m_up
            E[x + 11, 8:40, :] = E[x + 11, 8:40, :] * m_dn

        @pl.loop(1, 13)
        def _(i):
            q = E[i]
            diag = 3.0 * q + 0.5 * (E[i - 1] + E[i + 1] + side_sum(q))
            inside = q > 0
            w = jnp.where(inside, OMEGA / jnp.where(inside, diag, 1.0), 0.0)
            D[i] = diag
            W[i] = w
            PA[i] = w * R[i]

        def coupling(p, i):
            q, v = E[i], p[i]
            around = p[i - 1] + p[i + 1] + side_sum(v)
            return 0.5 * (q * around + E[i - 1] * p[i - 1] + E[i + 1] * p[i + 1] + side_sum(q * v))

        def relax(p, i):
            return (1.0 - OMEGA) * p[i] + W[i] * (R[i] + coupling(p, i))

        @pl.loop(2, 12)
        def _(i):
            PB[i] = relax(PA, i)

        def residual_row(x, carry):
            acc, con = carry
            i = x + 3
            res = (R[i] - D[i] * PB[i] + coupling(PB, i))[8:40]
            RES[x] = res
            return acc + res, con + E[i]

        acc, con = lax.fori_loop(
            0, 8, residual_row, (jnp.zeros((32, 256), F32), jnp.zeros((48, 256), F32))
        )

        sub48, lane48 = iota((48, 256), 0), iota((48, 256), 1)
        own = (sub48 >= 8) & (sub48 < 40)
        down = E[9] + E[10] + E[11] + E[12]
        up = E[1] + E[2] + E[3] + E[4]
        cross = jnp.where((sub48 >= 38) & (sub48 < 42), con, 0.0)
        back = jnp.where((sub48 >= 6) & (sub48 < 10), con, 0.0)
        ends = jnp.where(own & ((lane48 < 2) | (lane48 >= 254)), con, 0.0)
        down = jnp.where(own, down, 0.0)
        outflow = 0.25 * total_of(down + jnp.where(own, up, 0.0) + cross + back + ends)
        sums = [total_of(acc), outflow, 0.25 * total_of(down), 0.25 * total_of(cross)]
        my_lane = lax.rem(z, 2) * 64 + y * 8 + me1
        here = iota((1, 128), 1) == my_lane
        for k, value in enumerate(sums):
            M1[k : k + 1, :] = jnp.where(here, value, 0.0)

        gather1 = [remote(M1, G1.at[k], s1, r1, k, group1[k]) for k in range(n1 - 1)]
        gather2 = [remote(M2, G2.at[k], s2, r2, k, group2[k]) for k in range(ny - 1)]
        gather3 = [remote(M3, G3.at[k], s3, r3, k, group3[k]) for k in range(nz - 1)]
        for copy in gather1:
            copy.start()

        zero32 = jnp.zeros((32, 256), F32)
        for ref in (CC, FA, FB):
            ref[0] = zero32
            ref[5] = zero32

        @pl.loop(0, 4)
        def _(x):
            CR[x] = pair_sum(RES[2 * x] + RES[2 * x + 1])
            CC[x + 1] = 0.125 * pair_sum(E[2 * x + 3, 8:40, :] + E[2 * x + 4, 8:40, :])

        @pl.loop(1, 5)
        def _(i):
            q = CC[i]
            wt = OMEGA / (2.0 * (6.0 * q + CC[i - 1] + CC[i + 1] + tile_side_sum(q)))
            WT[i - 1] = wt
            FA[i] = wt * CR[i - 1]

        def tile_relax(f, i):
            q, v = CC[i], f[i]
            around = f[i - 1] + f[i + 1] + tile_side_sum(v)
            more = CC[i - 1] * f[i - 1] + CC[i + 1] * f[i + 1] + tile_side_sum(q * v)
            return (1.0 - OMEGA) * v + WT[i - 1] * (CR[i - 1] + 2.0 * (q * around + more))

        f, g = FA, FB
        for sweep in range(BLOCK_SWEEPS - 1):

            @pl.loop(1, 5)
            def _(i, f=f, g=g):
                g[i] = tile_relax(f, i)

            f, g = g, f

        tile_of_row = iota((32, 256), 0) // 8
        cloud = jnp.zeros((32, 256), F32)
        for t in range(4):
            cloud = jnp.where(tile_of_row == t, flag(route[0, t] >= 0), cloud)

        @pl.loop(0, 4)
        def _(x):
            fix = f[x + 1] * cloud
            Q[2 * x + 3, 8:40, :] = PB[2 * x + 3, 8:40, :] + fix
            Q[2 * x + 4, 8:40, :] = PB[2 * x + 4, 8:40, :] + fix

        for copy in gather1:
            copy.wait_recv()
        row = M1[...]
        for k in range(n1 - 1):
            row = row + G1[k]
        M2[...] = row
        for copy in gather2:
            copy.start()

        src_rows = {-1: slice(3, 5), 1: slice(9, 11)}
        dst_rows = {-1: slice(11, 13), 1: slice(1, 3)}
        src_cols = {-1: slice(8, 16), 1: slice(32, 40)}
        dst_cols = {-1: slice(40, 48), 1: slice(0, 8)}
        mid, band = slice(3, 11), slice(8, 40)
        fix_halo = []
        for k, sx in enumerate((-1, 1)):
            src, dst = Q.at[src_rows[sx], band, :], Q.at[dst_rows[sx], band, :]
            fix_halo.append(remote(src, dst, q_send, q_recv, k, near[k]))
        for k, sy in enumerate((-1, 1)):
            src, dst = Q.at[mid, src_cols[sy], :], Q.at[mid, dst_cols[sy], :]
            fix_halo.append(remote(src, dst, q_send, q_recv, 2 + k, near[2 + k]))
        for k, (sx, sy) in enumerate(CORNERS):
            src = Q.at[src_rows[sx], src_cols[sy], :]
            dst = Q.at[dst_rows[sx], dst_cols[sy], :]
            fix_halo.append(remote(src, dst, q_send, q_recv, 4 + k, corners[k]))
        for copy in fix_halo:
            copy.start()

        for copy in gather2:
            copy.wait_recv()
        row = M2[...]
        for k in range(ny - 1):
            row = row + G2[k]
        M3[...] = row
        for copy in gather3:
            copy.start()
        for copy in fix_halo:
            copy.wait_recv()

        sub, lane = iota((8, 128), 0), iota((8, 128), 1)
        tz = 2 * sub + lane // 64
        ty = (lane % 64) // 8
        tc = (lane % 8) // 2
        odd = lane % 2 == 1

        for copy in gather3:
            copy.wait_recv()
        table = [jnp.where(sub == lax.div(z, 2), M3[k : k + 1, :], 0.0) for k in range(4)]
        for j in range(nz - 1):
            from_z = lax.rem(z + nz - 1 - j, nz)
            at = sub == lax.div(from_z, 2)
            for k in range(4):
                table[k] = table[k] + jnp.where(at, G3[j, k : k + 1, :], 0.0)
        totals, outs, link_dn, link_cr = table

        def ahead(value, by):
            return pltpu.roll(value, (-by) % 128, 1)

        def shift_rows(value, by):
            return pltpu.roll(value, by % 8, 0)

        def next_parts(value):
            v63 = ahead(value, 63)
            return ahead(value, 1), v63, shift_rows(v63, -1), shift_rows(ahead(value, 71), half - 1)

        def prev_parts(value):
            v63 = ahead(value, -63)
            return (
                ahead(value, -1), v63, shift_rows(v63, 1), shift_rows(ahead(value, -71), 1 - half)
            )

        last = (ty == ny - 1) & (tz == nz - 1)
        first = (ty == 0) & (tz == 0)
        next_at = (
            ~odd,
            odd & (tz % 2 == 0),
            odd & (tz % 2 == 1) & (tz < nz - 1),
            odd & (tz == nz - 1) & ~last,
        )
        prev_at = (
            odd,
            ~odd & (tz % 2 == 1),
            ~odd & (tz % 2 == 0) & (tz > 0),
            ~odd & (tz == 0) & ~first,
        )
        link_up = jnp.zeros((8, 128), F32)
        held = (tz < nz) & (ty < ny) & (tc < n_cross)
        for at, part in zip(prev_at, prev_parts(link_dn)):
            link_up = jnp.where(at & held, part, link_up)
        link_bk = jnp.where((tc > 0) & held, ahead(link_cr, -2), 0.0)
        link_cr = jnp.where(tc < n_cross - 1, link_cr, 0.0)
        next_w = [jnp.where(at, link_dn, 0.0) for at in next_at]
        prev_w = [jnp.where(at, link_up, 0.0) for at in prev_at]

        def operate(value):
            image = outs * value - link_cr * ahead(value, 2) - link_bk * ahead(value, -2)
            for weight, part in zip(next_w, next_parts(value)):
                image = image - weight * part
            for weight, part in zip(prev_w, prev_parts(value)):
                image = image - weight * part
            return image

        def iterate(step, carry):
            answer, resid, search, norm_now = carry
            image = operate(search)
            alpha = norm_now / total_of(search * image)
            answer = answer + alpha * search
            resid = resid - alpha * image
            norm_next = total_of(resid * resid)
            search = resid + norm_next / norm_now * search
            return answer, resid, search, norm_next

        start = (jnp.zeros((8, 128), F32), totals, totals, total_of(totals * totals))
        answer = lax.fori_loop(0, COARSE_ITERS, iterate, start)[0]

        def brick(dd, cc):
            core_b, chip_b = lax.rem(dd, 2), lax.div(dd, 2)
            z_b, y_b = lax.rem(chip_b, nz), lax.div(chip_b, nz)
            at_lane = lax.rem(z_b, 2) * 64 + y_b * 8 + cc * 2 + core_b
            return total_of(jnp.where((sub == lax.div(z_b, 2)) & (lane == at_lane), answer, 0.0))

        col = iota((48, 256), 0)
        keep_col = jnp.where(col < 8, m_l, jnp.where(col < 40, 1.0, m_r))

        def brick_row(dd):
            left, mine, right = brick(dd, c_prev), brick(dd, c), brick(dd, c_next)
            return jnp.where(col < 8, left, jnp.where(col < 40, mine, right))

        for dd, lo, hi, keep in ((d_prev, 1, 3, m_up), (d, 3, 11, None), (d_next, 11, 13, m_dn)):
            add = brick_row(dd)
            mask = keep_col if keep is None else keep_col * keep

            @pl.loop(lo, hi)
            def _(i, add=add, mask=mask):
                PA[i] = (Q[i] + add) * mask

        @pl.loop(2, 12)
        def _(i):
            PB[i] = relax(PA, i)

        @pl.loop(3, 11)
        def _(i):
            out[i - 3] = relax(PB, i)[8:40]

        for copy in halo + gather1 + gather2 + gather3 + fix_halo:
            copy.wait_send()

    return kernel


def solution(mesh):
    n_down, n_cross = mesh.shape["down"], mesh.shape["cross"]
    nz = CHIPS_Z
    ny = n_down // (2 * nz)
    n1 = 2 * n_cross
    big = pltpu.VMEM((14, 48, 256), F32)
    dma = pltpu.SemaphoreType.DMA
    msg = pltpu.VMEM((4, 128), F32)

    def body(right_side, kappa, band_mask, tile_route):
        return pl.pallas_call(
            make_kernel(n_down, n_cross, nz),
            out_shape=jax.ShapeDtypeStruct(right_side.shape, F32),
            in_specs=[pl.BlockSpec(memory_space=pl.ANY)] * 3
            + [pl.BlockSpec(memory_space=pltpu.SMEM)],
            out_specs=pl.BlockSpec(memory_space=pltpu.VMEM),
            scratch_shapes=[
                big, big, pltpu.VMEM((8, 32, 256), jnp.int32), big, big, big, big, big,
                pltpu.VMEM((8, 32, 256), F32),
                pltpu.VMEM((4, 32, 256), F32), pltpu.VMEM((6, 32, 256), F32),
                pltpu.VMEM((4, 32, 256), F32), pltpu.VMEM((6, 32, 256), F32),
                pltpu.VMEM((6, 32, 256), F32),
                pltpu.VMEM((2, 8, 8, 256), F32), pltpu.VMEM((2, 8, 8, 256), F32),
                pltpu.VMEM((4, 2, 8, 256), F32),
                msg, pltpu.VMEM((n1 - 1, 4, 128), F32),
                msg, pltpu.VMEM((ny - 1, 4, 128), F32),
                msg, pltpu.VMEM((nz - 1, 4, 128), F32),
                dma((3,)), dma((10,)), dma((10,)), dma((8,)), dma((8,)),
                dma((n1 - 1,)), dma((n1 - 1,)), dma((ny - 1,)), dma((ny - 1,)),
                dma((nz - 1,)), dma((nz - 1,)),
            ],
            compiler_params=pltpu.CompilerParams(collective_id=0, has_side_effects=True),
            name="cycle",
        )(right_side, kappa, band_mask, tile_route)

    return jax.shard_map(
        body,
        mesh=mesh,
        in_specs=(
            P("down", "cross", None),
            P("down", "cross", None),
            P("down", "cross", None),
            P("down", "cross"),
        ),
        out_specs=P("down", "cross", None),
        check_vma=False,
    )
```

```python
import jax
import jax.numpy as jnp
from jax import lax
from jax.experimental import pallas as pl
from jax.experimental.pallas import tpu as pltpu
from jax.sharding import PartitionSpec as P

OMEGA = 0.8
BLOCK_SWEEPS = 4
COARSE_ITERS = 12
CHIPS_Z = 12

MESH = pl.DeviceIdType.MESH
CORNERS = ((-1, -1), (-1, 1), (1, -1), (1, 1))
F32 = jnp.float32


def iota(shape, dim):
    return lax.broadcasted_iota(jnp.int32, shape, dim)


def flag(cond):
    return jnp.where(cond, 1.0, 0.0).astype(F32)


def total_of(value):
    return jnp.sum(jnp.sum(value, axis=0, keepdims=True), axis=1, keepdims=True)


def shifted(value, by, tile=0):
    rows, lanes = value.shape
    row, lane = iota(value.shape, 0) % max(tile, 1), iota(value.shape, 1)
    back, ahead = pltpu.roll(value, by, 0), pltpu.roll(value, rows - by, 0)
    if tile:
        back = jnp.where(row >= by, back, 0.0)
        ahead = jnp.where(row < tile - by, ahead, 0.0)
    below = jnp.where(lane >= by, pltpu.roll(value, by, 1), 0.0)
    above = jnp.where(lane < lanes - by, pltpu.roll(value, lanes - by, 1), 0.0)
    return back, ahead, below, above


def rolled(value, by, rows_out):
    rows, lanes = value.shape
    return (
        pltpu.roll(value, by, 0)[:rows_out],
        pltpu.roll(value, rows - by, 0)[:rows_out],
        pltpu.roll(value[:rows_out], by, 1),
        pltpu.roll(value[:rows_out], lanes - by, 1),
    )


def pair_sum(value):
    rows, lanes = value.shape
    row, lane = iota(value.shape, 0), iota(value.shape, 1)
    value = value + jnp.where(row % 2 == 0, pltpu.roll(value, rows - 1, 0), pltpu.roll(value, 1, 0))
    return value + jnp.where(
        lane % 2 == 0, pltpu.roll(value, lanes - 1, 1), pltpu.roll(value, 1, 1)
    )


def make_kernel(n_down, n_cross, nz):
    ny = n_down // (2 * nz)
    half = nz // 2

    def kernel(
        rhs_hbm, kappa_hbm, mask_hbm, route, out,
        E, R, MK, D, W, PA, PB, Q, FX, FY, FZ, RES, CR, CC, WT, TX, TY, TZ, FA, FB,
        SX, LX, LK, QX, QK, M1, G1, M2, G2, M3, G3,
        load_sem, h_send, h_recv, q_send, q_recv,
        s1, r1, s2, r2, s3, r3,
    ):
        d = lax.axis_index("down")
        c = lax.axis_index("cross")
        core = lax.rem(d, 2)
        chip = lax.div(d, 2)
        z = lax.rem(chip, nz)
        y = lax.div(chip, nz)

        loads = [
            pltpu.make_async_copy(kappa_hbm, E.at[3:11, 0:32, :], load_sem.at[0]),
            pltpu.make_async_copy(mask_hbm, MK, load_sem.at[1]),
            pltpu.make_async_copy(rhs_hbm, R.at[3:11, 0:32, :], load_sem.at[2]),
        ]
        for load in loads:
            load.start()

        d_next, d_prev = lax.rem(d + 1, n_down), lax.rem(d + n_down - 1, n_down)
        c_next, c_prev = lax.rem(c + 1, n_cross), lax.rem(c + n_cross - 1, n_cross)
        near = [(d_prev, c), (d_next, c), (d, c_prev), (d, c_next)]
        corners = [
            (d_prev if sx < 0 else d_next, c_prev if sy < 0 else c_next) for sx, sy in CORNERS
        ]
        n1 = 2 * n_cross
        me1 = c * 2 + core
        group1 = []
        for k in range(1, n1):
            g = lax.rem(me1 + k, n1)
            group1.append((chip * 2 + lax.rem(g, 2), lax.div(g, 2)))
        group2 = [((lax.rem(y + k, ny) * nz + z) * 2 + core, c) for k in range(1, ny)]
        group3 = [((y * nz + lax.rem(z + k, nz)) * 2 + core, c) for k in range(1, nz)]

        barrier = pltpu.get_barrier_semaphore()
        peers = near + corners + group1 + group2 + group3
        for peer in peers:
            pl.semaphore_signal(barrier, inc=1, device_id=peer, device_id_type=MESH)

        m_up, m_dn = flag(d > 0), flag(d < n_down - 1)
        m_l, m_r = flag(c > 0), flag(c < n_cross - 1)

        zero8 = jnp.zeros((8, 256), F32)
        for i in (0, 13):
            E[i, 32:40, :] = zero8
        loads[0].wait()
        loads[1].wait()

        @pl.loop(0, 8)
        def _(x):
            kap = E[x + 3, 0:32, :]
            E[x + 3, 0:32, :] = jnp.where(MK[x] > 0, kap * 0.25, kap)

        loads[2].wait()
        sub8 = iota((8, 256), 0)

        @pl.loop(0, 8)
        def _(x):
            SX[0, x] = jnp.where(sub8 < 3, E[x + 3, 0:8, :], pltpu.roll(R[x + 3, 0:8, :], 3, 0))
            SX[1, x] = jnp.where(sub8 >= 5, E[x + 3, 24:32, :], pltpu.roll(R[x + 3, 24:32, :], 5, 0))

        pl.semaphore_wait(barrier, len(peers))

        def remote(src, dst, send, recv, k, peer):
            return pltpu.make_async_remote_copy(
                src_ref=src, dst_ref=dst, send_sem=send.at[k], recv_sem=recv.at[k],
                device_id=peer, device_id_type=MESH,
            )

        halo = [
            remote(E.at[3:6, 0:32, :], E.at[11:14, 0:32, :], h_send, h_recv, 0, near[0]),
            remote(E.at[8:11, 0:32, :], E.at[0:3, 0:32, :], h_send, h_recv, 1, near[1]),
            remote(SX.at[0], LX.at[1], h_send, h_recv, 2, near[2]),
            remote(SX.at[1], LX.at[0], h_send, h_recv, 3, near[3]),
            remote(R.at[3:5, 0:32, :], R.at[11:13, 0:32, :], h_send, h_recv, 4, near[0]),
            remote(R.at[9:11, 0:32, :], R.at[1:3, 0:32, :], h_send, h_recv, 5, near[1]),
        ]
        for k, (sx, sy) in enumerate(CORNERS):
            rows = slice(0, 2) if sx < 0 else slice(6, 8)
            src = SX.at[0 if sy < 0 else 1, rows]
            halo.append(remote(src, LK.at[3 - k], h_send, h_recv, 6 + k, corners[k]))
        for k in (6, 7, 8, 9, 0, 1, 2, 3, 4, 5):
            halo[k].start()
        for copy in halo:
            copy.wait_recv()

        def unpack(left, right, i, keep):
            right, left = right * (m_r * keep), left * (m_l * keep)
            E[i, 32:40, :] = jnp.where(sub8 < 3, right, jnp.where(sub8 >= 5, left, 0.0))
            right, left = pltpu.roll(right, 5, 0), pltpu.roll(left, 3, 0)
            R[i, 32:40, :] = jnp.where(sub8 < 2, right, jnp.where(sub8 >= 6, left, 0.0))

        @pl.loop(0, 8)
        def _(x):
            unpack(LX[0, x], LX[1, x], x + 3, 1.0)

        @pl.loop(0, 2)
        def _(x):
            unpack(LK[0, x], LK[1, x], x + 1, m_up)
            unpack(LK[2, x], LK[3, x], x + 11, m_dn)
            R[x + 1, 0:32, :] = R[x + 1, 0:32, :] * m_up
            R[x + 11, 0:32, :] = R[x + 11, 0:32, :] * m_dn

        @pl.loop(0, 3)
        def _(x):
            E[x, 0:32, :] = E[x, 0:32, :] * m_up
            E[x + 11, 0:32, :] = E[x + 11, 0:32, :] * m_dn

        lane40 = iota((40, 256), 1)

        @pl.loop(1, 13)
        def _(i):
            q = E[i]
            back, ahead_, below, above = shifted(q, 1)
            up, dn = E[i - 1], E[i + 1]
            diag = 3.0 * q + 0.5 * (((up + dn) + (back + ahead_)) + (below + above))
            inside = q > 0
            w = jnp.where(inside, OMEGA / jnp.where(inside, diag, 1.0), 0.0)
            FX[i] = 0.5 * (up + q)
            FX[i + 1] = 0.5 * (dn + q)
            FY[0, i] = 0.5 * (back + q)
            FY[1, i] = 0.5 * (ahead_ + q)
            FZ[0, i] = jnp.where(lane40 > 0, 0.5 * (below + q), 0.0)
            FZ[1, i] = jnp.where(lane40 < 255, 0.5 * (above + q), 0.0)
            D[i] = diag
            W[i] = w
            PA[i] = w * R[i]

        def coupling(p, i, n):
            back, ahead_, below, above = rolled(p[i], 1, n)
            along = FX[i, :n] * p[i - 1, :n] + FX[i + 1, :n] * p[i + 1, :n]
            across = FY[0, i, :n] * back + FY[1, i, :n] * ahead_
            return (along + across) + (FZ[0, i, :n] * below + FZ[1, i, :n] * above)

        def relax(p, i, n):
            return (1.0 - OMEGA) * p[i, :n] + W[i, :n] * (R[i, :n] + coupling(p, i, n))

        @pl.loop(2, 12)
        def _(i):
            PB[i] = relax(PA, i, 40)

        def residual_row(x, carry):
            acc, con = carry
            i = x + 3
            res = R[i, :32] - D[i, :32] * PB[i, :32] + coupling(PB, i, 32)
            RES[x] = res
            return acc + res, con + E[i]

        acc, con = lax.fori_loop(
            0, 8, residual_row, (jnp.zeros((32, 256), F32), jnp.zeros((40, 256), F32))
        )

        sub40 = iota((40, 256), 0)
        own = sub40 < 32
        down = E[9] + E[10] + E[11] + E[12]
        up = E[1] + E[2] + E[3] + E[4]
        cross = jnp.where((sub40 >= 30) & (sub40 < 34), con, 0.0)
        back = jnp.where((sub40 < 2) | (sub40 >= 38), con, 0.0)
        ends = jnp.where(own & ((lane40 < 2) | (lane40 >= 254)), con, 0.0)
        down = jnp.where(own, down, 0.0)
        outflow = 0.25 * total_of(down + jnp.where(own, up, 0.0) + cross + back + ends)
        sums = [total_of(acc), outflow, 0.25 * total_of(down), 0.25 * total_of(cross)]
        my_lane = lax.rem(z, 2) * 64 + y * 8 + me1
        here = iota((1, 128), 1) == my_lane
        for k, value in enumerate(sums):
            M1[k : k + 1, :] = jnp.where(here, value, 0.0)

        gather1 = [remote(M1, G1.at[k], s1, r1, k, group1[k]) for k in range(n1 - 1)]
        gather2 = [remote(M2, G2.at[k], s2, r2, k, group2[k]) for k in range(ny - 1)]
        gather3 = [remote(M3, G3.at[k], s3, r3, k, group3[k]) for k in range(nz - 1)]
        for copy in gather1:
            copy.start()

        zero32 = jnp.zeros((32, 256), F32)
        for ref in (CC, FA, FB):
            ref[0] = zero32
            ref[5] = zero32

        @pl.loop(0, 4)
        def _(x):
            CR[x] = pair_sum(RES[2 * x] + RES[2 * x + 1])
            CC[x + 1] = 0.125 * pair_sum(E[2 * x + 3, 0:32, :] + E[2 * x + 4, 0:32, :])

        lane32, row32 = iota((32, 256), 1), iota((32, 256), 0) % 8

        @pl.loop(1, 5)
        def _(i):
            q = CC[i]
            back, ahead_, below, above = shifted(q, 2, 8)
            up, dn = CC[i - 1], CC[i + 1]
            diag = 12.0 * q + 2.0 * (((up + dn) + (back + ahead_)) + (below + above))
            wt = OMEGA / diag
            TX[i] = 2.0 * (up + q)
            TX[i + 1] = 2.0 * (dn + q)
            TY[0, i] = jnp.where(row32 >= 2, 2.0 * (back + q), 0.0)
            TY[1, i] = jnp.where(row32 < 6, 2.0 * (ahead_ + q), 0.0)
            TZ[0, i] = jnp.where(lane32 >= 2, 2.0 * (below + q), 0.0)
            TZ[1, i] = jnp.where(lane32 < 254, 2.0 * (above + q), 0.0)
            WT[i] = wt
            FA[i] = wt * CR[i - 1]

        def tile_relax(f, i):
            v = f[i]
            back, ahead_, below, above = rolled(v, 2, 32)
            along = TX[i] * f[i - 1] + TX[i + 1] * f[i + 1]
            across = TY[0, i] * back + TY[1, i] * ahead_
            around = (along + across) + (TZ[0, i] * below + TZ[1, i] * above)
            return (1.0 - OMEGA) * v + WT[i] * (CR[i - 1] + around)

        f, g = FA, FB
        for sweep in range(BLOCK_SWEEPS - 1):

            @pl.loop(1, 5)
            def _(i, f=f, g=g):
                g[i] = tile_relax(f, i)

            f, g = g, f

        tile_of_row = iota((32, 256), 0) // 8
        cloud = jnp.zeros((32, 256), F32)
        for t in range(4):
            cloud = jnp.where(tile_of_row == t, flag(route[0, t] >= 0), cloud)

        @pl.loop(0, 4)
        def _(x):
            fix = f[x + 1] * cloud
            Q[2 * x + 3, 0:32, :] = PB[2 * x + 3, 0:32, :] + fix
            Q[2 * x + 4, 0:32, :] = PB[2 * x + 4, 0:32, :] + fix

        for copy in gather1:
            copy.wait_recv()
        row = M1[...]
        for k in range(n1 - 1):
            row = row + G1[k]
        M2[...] = row
        for copy in gather2:
            copy.start()

        src_rows = {-1: slice(3, 5), 1: slice(9, 11)}
        dst_rows = {-1: slice(11, 13), 1: slice(1, 3)}
        src_cols = {-1: slice(0, 8), 1: slice(24, 32)}
        mid, band = slice(3, 11), slice(0, 32)
        fix_halo = []
        for k, sx in enumerate((-1, 1)):
            src, dst = Q.at[src_rows[sx], band, :], Q.at[dst_rows[sx], band, :]
            fix_halo.append(remote(src, dst, q_send, q_recv, k, near[k]))
        for k, sy in enumerate((-1, 1)):
            src = Q.at[mid, src_cols[sy], :]
            fix_halo.append(remote(src, QX.at[1 - k], q_send, q_recv, 2 + k, near[2 + k]))
        for k, (sx, sy) in enumerate(CORNERS):
            src = Q.at[3 if sx < 0 else 10, src_cols[sy], :]
            fix_halo.append(remote(src, QK.at[3 - k], q_send, q_recv, 4 + k, corners[k]))
        for copy in fix_halo:
            copy.start()

        for copy in gather2:
            copy.wait_recv()
        row = M2[...]
        for k in range(ny - 1):
            row = row + G2[k]
        M3[...] = row
        for copy in gather3:
            copy.start()
        for copy in fix_halo:
            copy.wait_recv()

        sub, lane = iota((8, 128), 0), iota((8, 128), 1)
        tz = 2 * sub + lane // 64
        ty = (lane % 64) // 8
        tc = (lane % 8) // 2
        odd = lane % 2 == 1

        for copy in gather3:
            copy.wait_recv()
        table = [jnp.where(sub == lax.div(z, 2), M3[k : k + 1, :], 0.0) for k in range(4)]
        for j in range(nz - 1):
            from_z = lax.rem(z + nz - 1 - j, nz)
            at = sub == lax.div(from_z, 2)
            for k in range(4):
                table[k] = table[k] + jnp.where(at, G3[j, k : k + 1, :], 0.0)
        totals, outs, link_dn, link_cr = table

        def ahead(value, by):
            return pltpu.roll(value, (-by) % 128, 1)

        def shift_rows(value, by):
            return pltpu.roll(value, by % 8, 0)

        def next_parts(value):
            v63 = ahead(value, 63)
            return ahead(value, 1), v63, shift_rows(v63, -1), shift_rows(ahead(value, 71), half - 1)

        def prev_parts(value):
            v63 = ahead(value, -63)
            return (
                ahead(value, -1), v63, shift_rows(v63, 1), shift_rows(ahead(value, -71), 1 - half)
            )

        last = (ty == ny - 1) & (tz == nz - 1)
        first = (ty == 0) & (tz == 0)
        next_at = (
            ~odd,
            odd & (tz % 2 == 0),
            odd & (tz % 2 == 1) & (tz < nz - 1),
            odd & (tz == nz - 1) & ~last,
        )
        prev_at = (
            odd,
            ~odd & (tz % 2 == 1),
            ~odd & (tz % 2 == 0) & (tz > 0),
            ~odd & (tz == 0) & ~first,
        )
        link_up = jnp.zeros((8, 128), F32)
        held = (tz < nz) & (ty < ny) & (tc < n_cross)
        for at, part in zip(prev_at, prev_parts(link_dn)):
            link_up = jnp.where(at & held, part, link_up)
        link_bk = jnp.where((tc > 0) & held, ahead(link_cr, -2), 0.0)
        link_cr = jnp.where(tc < n_cross - 1, link_cr, 0.0)
        next_w = [jnp.where(at, link_dn, 0.0) for at in next_at]
        prev_w = [jnp.where(at, link_up, 0.0) for at in prev_at]

        def operate(value):
            image = outs * value - link_cr * ahead(value, 2) - link_bk * ahead(value, -2)
            for weight, part in zip(next_w, next_parts(value)):
                image = image - weight * part
            for weight, part in zip(prev_w, prev_parts(value)):
                image = image - weight * part
            return image

        def iterate(step, carry):
            answer, resid, search, norm_now = carry
            image = operate(search)
            alpha = norm_now / total_of(search * image)
            answer = answer + alpha * search
            resid = resid - alpha * image
            norm_next = total_of(resid * resid)
            search = resid + norm_next / norm_now * search
            return answer, resid, search, norm_next

        start = (jnp.zeros((8, 128), F32), totals, totals, total_of(totals * totals))
        answer = lax.fori_loop(0, COARSE_ITERS, iterate, start)[0]

        def brick(dd, cc):
            core_b, chip_b = lax.rem(dd, 2), lax.div(dd, 2)
            z_b, y_b = lax.rem(chip_b, nz), lax.div(chip_b, nz)
            at_lane = lax.rem(z_b, 2) * 64 + y_b * 8 + cc * 2 + core_b
            return total_of(jnp.where((sub == lax.div(z_b, 2)) & (lane == at_lane), answer, 0.0))

        for dd, lo, hi, keep in ((d_prev, 1, 3, m_up), (d, 3, 11, 1.0), (d_next, 11, 13, m_dn)):
            left, own_, right = brick(dd, c_prev), brick(dd, c), brick(dd, c_next)

            @pl.loop(lo, hi)
            def _(i, own_=own_, keep=keep):
                PA[i, 0:32, :] = (Q[i, 0:32, :] + own_) * keep

            def beside(side_l, side_r, left=left, right=right, keep=keep):
                tile = jnp.where(sub8 < 4, (side_r + right) * m_r, (side_l + left) * m_l)
                return tile * keep

            if lo == 3:

                @pl.loop(0, 8)
                def _(x, beside=beside):
                    PA[x + 3, 32:40, :] = beside(QX[0, x], QX[1, x])

            elif lo == 1:
                PA[1, 32:40, :] = zero8
                PA[2, 32:40, :] = beside(QK[0], QK[1])
            else:
                PA[11, 32:40, :] = beside(QK[2], QK[3])
                PA[12, 32:40, :] = zero8

        @pl.loop(2, 12)
        def _(i):
            PB[i] = relax(PA, i, 40)

        @pl.loop(3, 11)
        def _(i):
            out[i - 3] = relax(PB, i, 32)

        for copy in halo + gather1 + gather2 + gather3 + fix_halo:
            copy.wait_send()

    return kernel


def solution(mesh):
    n_down, n_cross = mesh.shape["down"], mesh.shape["cross"]
    nz = CHIPS_Z
    ny = n_down // (2 * nz)
    n1 = 2 * n_cross
    big = pltpu.VMEM((14, 40, 256), F32)
    two = pltpu.VMEM((2, 14, 40, 256), F32)
    coarse = pltpu.VMEM((6, 32, 256), F32)
    coarse2 = pltpu.VMEM((2, 6, 32, 256), F32)
    dma = pltpu.SemaphoreType.DMA
    msg = pltpu.VMEM((4, 128), F32)

    def body(right_side, kappa, band_mask, tile_route):
        return pl.pallas_call(
            make_kernel(n_down, n_cross, nz),
            out_shape=pltpu.VMEM(right_side.shape, F32),
            in_specs=[pl.BlockSpec(memory_space=pl.ANY)] * 3
            + [pl.BlockSpec(memory_space=pltpu.SMEM)],
            out_specs=pl.BlockSpec(memory_space=pltpu.VMEM),
            scratch_shapes=[
                big, big, pltpu.VMEM((8, 32, 256), jnp.int32), big, big, big, big, big,
                big, two, two,
                pltpu.VMEM((8, 32, 256), F32),
                pltpu.VMEM((4, 32, 256), F32), coarse, coarse, coarse, coarse2, coarse2,
                coarse, coarse,
                pltpu.VMEM((2, 8, 8, 256), F32), pltpu.VMEM((2, 8, 8, 256), F32),
                pltpu.VMEM((4, 2, 8, 256), F32),
                pltpu.VMEM((2, 8, 8, 256), F32), pltpu.VMEM((4, 8, 256), F32),
                msg, pltpu.VMEM((n1 - 1, 4, 128), F32),
                msg, pltpu.VMEM((ny - 1, 4, 128), F32),
                msg, pltpu.VMEM((nz - 1, 4, 128), F32),
                dma((3,)), dma((10,)), dma((10,)), dma((8,)), dma((8,)),
                dma((n1 - 1,)), dma((n1 - 1,)), dma((ny - 1,)), dma((ny - 1,)),
                dma((nz - 1,)), dma((nz - 1,)),
            ],
            compiler_params=pltpu.CompilerParams(collective_id=0, has_side_effects=True),
            name="cycle",
        )(right_side, kappa, band_mask, tile_route)

    return jax.shard_map(
        body,
        mesh=mesh,
        in_specs=(
            P("down", "cross", None),
            P("down", "cross", None),
            P("down", "cross", None),
            P("down", "cross"),
        ),
        out_specs=P("down", "cross", None),
        check_vma=False,
    )
```

```python
import jax
import jax.numpy as jnp
from jax import lax
from jax.experimental import pallas as pl
from jax.experimental.pallas import tpu as pltpu
from jax.sharding import PartitionSpec as P

OMEGA = 0.8
BLOCK_SWEEPS = 4
COARSE_ITERS = 12
CHIPS_Z = 12

MESH = pl.DeviceIdType.MESH
CORNERS = ((-1, -1), (-1, 1), (1, -1), (1, 1))
F32 = jnp.float32


def iota(shape, dim):
    return lax.broadcasted_iota(jnp.int32, shape, dim)


def flag(cond):
    return jnp.where(cond, 1.0, 0.0).astype(F32)


def total_of(value):
    return jnp.sum(jnp.sum(value, axis=0, keepdims=True), axis=1, keepdims=True)


def shifted(value, by, tile=0):
    rows, lanes = value.shape
    row, lane = iota(value.shape, 0) % max(tile, 1), iota(value.shape, 1)
    back, ahead = pltpu.roll(value, by, 0), pltpu.roll(value, rows - by, 0)
    if tile:
        back = jnp.where(row >= by, back, 0.0)
        ahead = jnp.where(row < tile - by, ahead, 0.0)
    below = jnp.where(lane >= by, pltpu.roll(value, by, 1), 0.0)
    above = jnp.where(lane < lanes - by, pltpu.roll(value, lanes - by, 1), 0.0)
    return back, ahead, below, above


def rolled(value, by, rows_out):
    rows, lanes = value.shape
    return (
        pltpu.roll(value, by, 0)[:rows_out],
        pltpu.roll(value, rows - by, 0)[:rows_out],
        pltpu.roll(value[:rows_out], by, 1),
        pltpu.roll(value[:rows_out], lanes - by, 1),
    )


def pair_sum(value):
    rows, lanes = value.shape
    row, lane = iota(value.shape, 0), iota(value.shape, 1)
    value = value + jnp.where(row % 2 == 0, pltpu.roll(value, rows - 1, 0), pltpu.roll(value, 1, 0))
    return value + jnp.where(
        lane % 2 == 0, pltpu.roll(value, lanes - 1, 1), pltpu.roll(value, 1, 1)
    )


def make_kernel(n_down, n_cross, nz):
    ny = n_down // (2 * nz)
    half = nz // 2

    def kernel(
        rhs_hbm, kappa_hbm, mask_hbm, route, out,
        E, R, MK, D, W, PA, PB, Q, FX, FY, FZ, RES, CR, CC, WT, TX, TY, TZ, FA, FB,
        SX, LX, LK, QX, QK, M1, G1, M2, G2, M3, G3,
        load_sem, h_send, h_recv, q_send, q_recv,
        s1, r1, s2, r2, s3, r3, chain,
    ):
        d = lax.axis_index("down")
        c = lax.axis_index("cross")
        core = lax.rem(d, 2)
        chip = lax.div(d, 2)
        z = lax.rem(chip, nz)
        y = lax.div(chip, nz)

        loads = [
            pltpu.make_async_copy(kappa_hbm, E.at[3:11, 0:32, :], load_sem.at[0]),
            pltpu.make_async_copy(mask_hbm, MK, load_sem.at[1]),
            pltpu.make_async_copy(rhs_hbm, R.at[3:11, 0:32, :], load_sem.at[2]),
        ]
        for load in loads:
            load.start()

        d_next, d_prev = lax.rem(d + 1, n_down), lax.rem(d + n_down - 1, n_down)
        c_next, c_prev = lax.rem(c + 1, n_cross), lax.rem(c + n_cross - 1, n_cross)
        near = [(d_prev, c), (d_next, c), (d, c_prev), (d, c_next)]
        corners = [
            (d_prev if sx < 0 else d_next, c_prev if sy < 0 else c_next) for sx, sy in CORNERS
        ]
        n1 = 2 * n_cross
        me1 = c * 2 + core
        group1 = []
        for k in range(1, n1):
            g = lax.rem(me1 + k, n1)
            group1.append((chip * 2 + lax.rem(g, 2), lax.div(g, 2)))
        group2 = [((lax.rem(y + k, ny) * nz + z) * 2 + core, c) for k in range(1, ny)]
        group3 = [((y * nz + lax.rem(z + k, nz)) * 2 + core, c) for k in range(1, nz)]

        barrier = pltpu.get_barrier_semaphore()
        def at_z(by):
            return ((y * nz + lax.rem(z + nz + by, nz)) * 2 + core, c)

        def at_y(by):
            return ((lax.rem(y + ny + by, ny) * nz + z) * 2 + core, c)

        beside = [at_z(1), at_z(-1), at_y(1), at_y(-1)]
        rounds = [beside, [at_z(2), at_z(-2), at_y(2), at_y(-2)], [at_z(2), at_z(-2)]]
        peers = near + corners + group1 + beside
        for peer in peers:
            pl.semaphore_signal(barrier, inc=1, device_id=peer, device_id_type=MESH)

        m_up, m_dn = flag(d > 0), flag(d < n_down - 1)
        m_l, m_r = flag(c > 0), flag(c < n_cross - 1)

        zero8 = jnp.zeros((8, 256), F32)
        for i in (0, 13):
            E[i, 32:40, :] = zero8
        loads[0].wait()
        loads[1].wait()

        @pl.loop(0, 8)
        def _(x):
            kap = E[x + 3, 0:32, :]
            E[x + 3, 0:32, :] = jnp.where(MK[x] > 0, kap * 0.25, kap)

        loads[2].wait()
        sub8 = iota((8, 256), 0)

        @pl.loop(0, 8)
        def _(x):
            SX[0, x] = jnp.where(sub8 < 3, E[x + 3, 0:8, :], pltpu.roll(R[x + 3, 0:8, :], 3, 0))
            SX[1, x] = jnp.where(sub8 >= 5, E[x + 3, 24:32, :], pltpu.roll(R[x + 3, 24:32, :], 5, 0))

        pl.semaphore_wait(barrier, len(peers))

        def announce(k):
            for peer in rounds[k]:
                pl.semaphore_signal(chain.at[k], inc=1, device_id=peer, device_id_type=MESH)

        def heard(k):
            pl.semaphore_wait(chain.at[k], len(rounds[k]))

        def remote(src, dst, send, recv, k, peer):
            return pltpu.make_async_remote_copy(
                src_ref=src, dst_ref=dst, send_sem=send.at[k], recv_sem=recv.at[k],
                device_id=peer, device_id_type=MESH,
            )

        halo = [
            remote(E.at[3:6, 0:32, :], E.at[11:14, 0:32, :], h_send, h_recv, 0, near[0]),
            remote(E.at[8:11, 0:32, :], E.at[0:3, 0:32, :], h_send, h_recv, 1, near[1]),
            remote(SX.at[0], LX.at[1], h_send, h_recv, 2, near[2]),
            remote(SX.at[1], LX.at[0], h_send, h_recv, 3, near[3]),
            remote(R.at[3:5, 0:32, :], R.at[11:13, 0:32, :], h_send, h_recv, 4, near[0]),
            remote(R.at[9:11, 0:32, :], R.at[1:3, 0:32, :], h_send, h_recv, 5, near[1]),
        ]
        for k, (sx, sy) in enumerate(CORNERS):
            rows = slice(0, 2) if sx < 0 else slice(6, 8)
            src = SX.at[0 if sy < 0 else 1, rows]
            halo.append(remote(src, LK.at[3 - k], h_send, h_recv, 6 + k, corners[k]))
        for k in (6, 7, 8, 9, 0, 1, 2, 3, 4, 5):
            halo[k].start()
        announce(0)
        for copy in halo:
            copy.wait_recv()
        heard(0)
        announce(1)

        def unpack(left, right, i, keep):
            right, left = right * (m_r * keep), left * (m_l * keep)
            E[i, 32:40, :] = jnp.where(sub8 < 3, right, jnp.where(sub8 >= 5, left, 0.0))
            right, left = pltpu.roll(right, 5, 0), pltpu.roll(left, 3, 0)
            R[i, 32:40, :] = jnp.where(sub8 < 2, right, jnp.where(sub8 >= 6, left, 0.0))

        @pl.loop(0, 8)
        def _(x):
            unpack(LX[0, x], LX[1, x], x + 3, 1.0)

        @pl.loop(0, 2)
        def _(x):
            unpack(LK[0, x], LK[1, x], x + 1, m_up)
            unpack(LK[2, x], LK[3, x], x + 11, m_dn)
            R[x + 1, 0:32, :] = R[x + 1, 0:32, :] * m_up
            R[x + 11, 0:32, :] = R[x + 11, 0:32, :] * m_dn

        @pl.loop(0, 3)
        def _(x):
            E[x, 0:32, :] = E[x, 0:32, :] * m_up
            E[x + 11, 0:32, :] = E[x + 11, 0:32, :] * m_dn

        lane40 = iota((40, 256), 1)

        @pl.loop(1, 13)
        def _(i):
            q = E[i]
            back, ahead_, below, above = shifted(q, 1)
            up, dn = E[i - 1], E[i + 1]
            diag = 3.0 * q + 0.5 * (((up + dn) + (back + ahead_)) + (below + above))
            inside = q > 0
            w = jnp.where(inside, OMEGA / jnp.where(inside, diag, 1.0), 0.0)
            FX[i] = 0.5 * (up + q)
            FX[i + 1] = 0.5 * (dn + q)
            FY[0, i] = 0.5 * (back + q)
            FY[1, i] = 0.5 * (ahead_ + q)
            FZ[0, i] = jnp.where(lane40 > 0, 0.5 * (below + q), 0.0)
            FZ[1, i] = jnp.where(lane40 < 255, 0.5 * (above + q), 0.0)
            D[i] = diag
            W[i] = w
            PA[i] = w * R[i]

        heard(1)
        announce(2)

        def coupling(p, i, n):
            back, ahead_, below, above = rolled(p[i], 1, n)
            along = FX[i, :n] * p[i - 1, :n] + FX[i + 1, :n] * p[i + 1, :n]
            across = FY[0, i, :n] * back + FY[1, i, :n] * ahead_
            return (along + across) + (FZ[0, i, :n] * below + FZ[1, i, :n] * above)

        def relax(p, i, n):
            return (1.0 - OMEGA) * p[i, :n] + W[i, :n] * (R[i, :n] + coupling(p, i, n))

        @pl.loop(2, 12)
        def _(i):
            PB[i] = relax(PA, i, 40)

        def residual_row(x, carry):
            acc, con = carry
            i = x + 3
            res = R[i, :32] - D[i, :32] * PB[i, :32] + coupling(PB, i, 32)
            RES[x] = res
            return acc + res, con + E[i]

        acc, con = lax.fori_loop(
            0, 8, residual_row, (jnp.zeros((32, 256), F32), jnp.zeros((40, 256), F32))
        )

        sub40 = iota((40, 256), 0)
        own = sub40 < 32
        down = E[9] + E[10] + E[11] + E[12]
        up = E[1] + E[2] + E[3] + E[4]
        cross = jnp.where((sub40 >= 30) & (sub40 < 34), con, 0.0)
        back = jnp.where((sub40 < 2) | (sub40 >= 38), con, 0.0)
        ends = jnp.where(own & ((lane40 < 2) | (lane40 >= 254)), con, 0.0)
        down = jnp.where(own, down, 0.0)
        outflow = 0.25 * total_of(down + jnp.where(own, up, 0.0) + cross + back + ends)
        sums = [total_of(acc), outflow, 0.25 * total_of(down), 0.25 * total_of(cross)]
        my_lane = lax.rem(z, 2) * 64 + y * 8 + me1
        here = iota((1, 128), 1) == my_lane
        for k, value in enumerate(sums):
            M1[k : k + 1, :] = jnp.where(here, value, 0.0)

        gather1 = [remote(M1, G1.at[k], s1, r1, k, group1[k]) for k in range(n1 - 1)]
        gather2 = [remote(M2, G2.at[k], s2, r2, k, group2[k]) for k in range(ny - 1)]
        gather3 = [remote(M3, G3.at[k], s3, r3, k, group3[k]) for k in range(nz - 1)]
        for copy in gather1:
            copy.start()

        zero32 = jnp.zeros((32, 256), F32)
        for ref in (CC, FA, FB):
            ref[0] = zero32
            ref[5] = zero32

        @pl.loop(0, 4)
        def _(x):
            CR[x] = pair_sum(RES[2 * x] + RES[2 * x + 1])
            CC[x + 1] = 0.125 * pair_sum(E[2 * x + 3, 0:32, :] + E[2 * x + 4, 0:32, :])

        lane32, row32 = iota((32, 256), 1), iota((32, 256), 0) % 8

        @pl.loop(1, 5)
        def _(i):
            q = CC[i]
            back, ahead_, below, above = shifted(q, 2, 8)
            up, dn = CC[i - 1], CC[i + 1]
            diag = 12.0 * q + 2.0 * (((up + dn) + (back + ahead_)) + (below + above))
            wt = OMEGA / diag
            TX[i] = 2.0 * (up + q)
            TX[i + 1] = 2.0 * (dn + q)
            TY[0, i] = jnp.where(row32 >= 2, 2.0 * (back + q), 0.0)
            TY[1, i] = jnp.where(row32 < 6, 2.0 * (ahead_ + q), 0.0)
            TZ[0, i] = jnp.where(lane32 >= 2, 2.0 * (below + q), 0.0)
            TZ[1, i] = jnp.where(lane32 < 254, 2.0 * (above + q), 0.0)
            WT[i] = wt
            FA[i] = wt * CR[i - 1]

        def tile_relax(f, i):
            v = f[i]
            back, ahead_, below, above = rolled(v, 2, 32)
            along = TX[i] * f[i - 1] + TX[i + 1] * f[i + 1]
            across = TY[0, i] * back + TY[1, i] * ahead_
            around = (along + across) + (TZ[0, i] * below + TZ[1, i] * above)
            return (1.0 - OMEGA) * v + WT[i] * (CR[i - 1] + around)

        f, g = FA, FB
        for sweep in range(BLOCK_SWEEPS - 1):

            @pl.loop(1, 5)
            def _(i, f=f, g=g):
                g[i] = tile_relax(f, i)

            f, g = g, f

        tile_of_row = iota((32, 256), 0) // 8
        cloud = jnp.zeros((32, 256), F32)
        for t in range(4):
            cloud = jnp.where(tile_of_row == t, flag(route[0, t] >= 0), cloud)

        @pl.loop(0, 4)
        def _(x):
            fix = f[x + 1] * cloud
            Q[2 * x + 3, 0:32, :] = PB[2 * x + 3, 0:32, :] + fix
            Q[2 * x + 4, 0:32, :] = PB[2 * x + 4, 0:32, :] + fix

        for copy in gather1:
            copy.wait_recv()
        row = M1[...]
        for k in range(n1 - 1):
            row = row + G1[k]
        M2[...] = row
        for copy in gather2:
            copy.start()

        src_rows = {-1: slice(3, 5), 1: slice(9, 11)}
        dst_rows = {-1: slice(11, 13), 1: slice(1, 3)}
        src_cols = {-1: slice(0, 8), 1: slice(24, 32)}
        mid, band = slice(3, 11), slice(0, 32)
        fix_halo = []
        for k, sx in enumerate((-1, 1)):
            src, dst = Q.at[src_rows[sx], band, :], Q.at[dst_rows[sx], band, :]
            fix_halo.append(remote(src, dst, q_send, q_recv, k, near[k]))
        for k, sy in enumerate((-1, 1)):
            src = Q.at[mid, src_cols[sy], :]
            fix_halo.append(remote(src, QX.at[1 - k], q_send, q_recv, 2 + k, near[2 + k]))
        for k, (sx, sy) in enumerate(CORNERS):
            src = Q.at[3 if sx < 0 else 10, src_cols[sy], :]
            fix_halo.append(remote(src, QK.at[3 - k], q_send, q_recv, 4 + k, corners[k]))
        for copy in fix_halo:
            copy.start()

        for copy in gather2:
            copy.wait_recv()
        row = M2[...]
        for k in range(ny - 1):
            row = row + G2[k]
        M3[...] = row
        heard(2)
        for copy in gather3:
            copy.start()
        for copy in fix_halo:
            copy.wait_recv()

        sub, lane = iota((8, 128), 0), iota((8, 128), 1)
        tz = 2 * sub + lane // 64
        ty = (lane % 64) // 8
        tc = (lane % 8) // 2
        odd = lane % 2 == 1

        for copy in gather3:
            copy.wait_recv()
        table = [jnp.where(sub == lax.div(z, 2), M3[k : k + 1, :], 0.0) for k in range(4)]
        for j in range(nz - 1):
            from_z = lax.rem(z + nz - 1 - j, nz)
            at = sub == lax.div(from_z, 2)
            for k in range(4):
                table[k] = table[k] + jnp.where(at, G3[j, k : k + 1, :], 0.0)
        totals, outs, link_dn, link_cr = table

        def ahead(value, by):
            return pltpu.roll(value, (-by) % 128, 1)

        def shift_rows(value, by):
            return pltpu.roll(value, by % 8, 0)

        def next_parts(value):
            v63 = ahead(value, 63)
            return ahead(value, 1), v63, shift_rows(v63, -1), shift_rows(ahead(value, 71), half - 1)

        def prev_parts(value):
            v63 = ahead(value, -63)
            return (
                ahead(value, -1), v63, shift_rows(v63, 1), shift_rows(ahead(value, -71), 1 - half)
            )

        last = (ty == ny - 1) & (tz == nz - 1)
        first = (ty == 0) & (tz == 0)
        next_at = (
            ~odd,
            odd & (tz % 2 == 0),
            odd & (tz % 2 == 1) & (tz < nz - 1),
            odd & (tz == nz - 1) & ~last,
        )
        prev_at = (
            odd,
            ~odd & (tz % 2 == 1),
            ~odd & (tz % 2 == 0) & (tz > 0),
            ~odd & (tz == 0) & ~first,
        )
        link_up = jnp.zeros((8, 128), F32)
        held = (tz < nz) & (ty < ny) & (tc < n_cross)
        for at, part in zip(prev_at, prev_parts(link_dn)):
            link_up = jnp.where(at & held, part, link_up)
        link_bk = jnp.where((tc > 0) & held, ahead(link_cr, -2), 0.0)
        link_cr = jnp.where(tc < n_cross - 1, link_cr, 0.0)
        next_w = [jnp.where(at, link_dn, 0.0) for at in next_at]
        prev_w = [jnp.where(at, link_up, 0.0) for at in prev_at]

        def operate(value):
            image = outs * value - link_cr * ahead(value, 2) - link_bk * ahead(value, -2)
            for weight, part in zip(next_w, next_parts(value)):
                image = image - weight * part
            for weight, part in zip(prev_w, prev_parts(value)):
                image = image - weight * part
            return image

        def iterate(step, carry):
            answer, resid, search, norm_now = carry
            image = operate(search)
            alpha = norm_now / total_of(search * image)
            answer = answer + alpha * search
            resid = resid - alpha * image
            norm_next = total_of(resid * resid)
            search = resid + norm_next / norm_now * search
            return answer, resid, search, norm_next

        start = (jnp.zeros((8, 128), F32), totals, totals, total_of(totals * totals))
        answer = lax.fori_loop(0, COARSE_ITERS, iterate, start)[0]

        def brick(dd, cc):
            core_b, chip_b = lax.rem(dd, 2), lax.div(dd, 2)
            z_b, y_b = lax.rem(chip_b, nz), lax.div(chip_b, nz)
            at_lane = lax.rem(z_b, 2) * 64 + y_b * 8 + cc * 2 + core_b
            return total_of(jnp.where((sub == lax.div(z_b, 2)) & (lane == at_lane), answer, 0.0))

        for dd, lo, hi, keep in ((d_prev, 1, 3, m_up), (d, 3, 11, 1.0), (d_next, 11, 13, m_dn)):
            left, own_, right = brick(dd, c_prev), brick(dd, c), brick(dd, c_next)

            @pl.loop(lo, hi)
            def _(i, own_=own_, keep=keep):
                PA[i, 0:32, :] = (Q[i, 0:32, :] + own_) * keep

            def beside(side_l, side_r, left=left, right=right, keep=keep):
                tile = jnp.where(sub8 < 4, (side_r + right) * m_r, (side_l + left) * m_l)
                return tile * keep

            if lo == 3:

                @pl.loop(0, 8)
                def _(x, beside=beside):
                    PA[x + 3, 32:40, :] = beside(QX[0, x], QX[1, x])

            elif lo == 1:
                PA[1, 32:40, :] = zero8
                PA[2, 32:40, :] = beside(QK[0], QK[1])
            else:
                PA[11, 32:40, :] = beside(QK[2], QK[3])
                PA[12, 32:40, :] = zero8

        @pl.loop(2, 12)
        def _(i):
            PB[i] = relax(PA, i, 40)

        @pl.loop(3, 11)
        def _(i):
            out[i - 3] = relax(PB, i, 32)

        for copy in halo + gather1 + gather2 + gather3 + fix_halo:
            copy.wait_send()

    return kernel


def solution(mesh):
    n_down, n_cross = mesh.shape["down"], mesh.shape["cross"]
    nz = CHIPS_Z
    ny = n_down // (2 * nz)
    n1 = 2 * n_cross
    big = pltpu.VMEM((14, 40, 256), F32)
    two = pltpu.VMEM((2, 14, 40, 256), F32)
    coarse = pltpu.VMEM((6, 32, 256), F32)
    coarse2 = pltpu.VMEM((2, 6, 32, 256), F32)
    dma = pltpu.SemaphoreType.DMA
    msg = pltpu.VMEM((4, 128), F32)

    def body(right_side, kappa, band_mask, tile_route):
        return pl.pallas_call(
            make_kernel(n_down, n_cross, nz),
            out_shape=pltpu.VMEM(right_side.shape, F32),
            in_specs=[pl.BlockSpec(memory_space=pl.ANY)] * 3
            + [pl.BlockSpec(memory_space=pltpu.SMEM)],
            out_specs=pl.BlockSpec(memory_space=pltpu.VMEM),
            scratch_shapes=[
                big, big, pltpu.VMEM((8, 32, 256), jnp.int32), big, big, big, big, big,
                big, two, two,
                pltpu.VMEM((8, 32, 256), F32),
                pltpu.VMEM((4, 32, 256), F32), coarse, coarse, coarse, coarse2, coarse2,
                coarse, coarse,
                pltpu.VMEM((2, 8, 8, 256), F32), pltpu.VMEM((2, 8, 8, 256), F32),
                pltpu.VMEM((4, 2, 8, 256), F32),
                pltpu.VMEM((2, 8, 8, 256), F32), pltpu.VMEM((4, 8, 256), F32),
                msg, pltpu.VMEM((n1 - 1, 4, 128), F32),
                msg, pltpu.VMEM((ny - 1, 4, 128), F32),
                msg, pltpu.VMEM((nz - 1, 4, 128), F32),
                dma((3,)), dma((10,)), dma((10,)), dma((8,)), dma((8,)),
                dma((n1 - 1,)), dma((n1 - 1,)), dma((ny - 1,)), dma((ny - 1,)),
                dma((nz - 1,)), dma((nz - 1,)), pltpu.SemaphoreType.REGULAR((3,)),
            ],
            compiler_params=pltpu.CompilerParams(collective_id=0, has_side_effects=True),
            name="cycle",
        )(right_side, kappa, band_mask, tile_route)

    return jax.shard_map(
        body,
        mesh=mesh,
        in_specs=(
            P("down", "cross", None),
            P("down", "cross", None),
            P("down", "cross", None),
            P("down", "cross"),
        ),
        out_specs=P("down", "cross", None),
        check_vma=False,
    )
```

```python
import jax
import jax.numpy as jnp
from jax import lax
from jax.experimental import pallas as pl
from jax.experimental.pallas import tpu as pltpu
from jax.sharding import PartitionSpec as P

OMEGA = 0.8
BLOCK_SWEEPS = 4
COARSE_ITERS = 12
CHIPS_Z = 12

MESH = pl.DeviceIdType.MESH
CORNERS = ((-1, -1), (-1, 1), (1, -1), (1, 1))
F32 = jnp.float32


def iota(shape, dim):
    return lax.broadcasted_iota(jnp.int32, shape, dim)


def flag(cond):
    return jnp.where(cond, 1.0, 0.0).astype(F32)


def total_of(value):
    return jnp.sum(jnp.sum(value, axis=0, keepdims=True), axis=1, keepdims=True)


def shifted(value, by, tile=0):
    rows, lanes = value.shape
    row, lane = iota(value.shape, 0) % max(tile, 1), iota(value.shape, 1)
    back, ahead = pltpu.roll(value, by, 0), pltpu.roll(value, rows - by, 0)
    if tile:
        back = jnp.where(row >= by, back, 0.0)
        ahead = jnp.where(row < tile - by, ahead, 0.0)
    below = jnp.where(lane >= by, pltpu.roll(value, by, 1), 0.0)
    above = jnp.where(lane < lanes - by, pltpu.roll(value, lanes - by, 1), 0.0)
    return back, ahead, below, above


def rolled(value, by, rows_out):
    rows, lanes = value.shape
    return (
        pltpu.roll(value, by, 0)[:rows_out],
        pltpu.roll(value, rows - by, 0)[:rows_out],
        pltpu.roll(value[:rows_out], by, 1),
        pltpu.roll(value[:rows_out], lanes - by, 1),
    )


def pair_sum(value):
    rows, lanes = value.shape
    row, lane = iota(value.shape, 0), iota(value.shape, 1)
    value = value + jnp.where(row % 2 == 0, pltpu.roll(value, rows - 1, 0), pltpu.roll(value, 1, 0))
    return value + jnp.where(
        lane % 2 == 0, pltpu.roll(value, lanes - 1, 1), pltpu.roll(value, 1, 1)
    )


def make_kernel(n_down, n_cross, nz):
    ny = n_down // (2 * nz)
    half = nz // 2

    def kernel(
        rhs_hbm, kappa_hbm, mask_hbm, route, out,
        E, R, MK, D, W, PA, PB, Q, FX, FY, FZ, RES, CR, CC, WT, TX, TY, TZ, FA, FB,
        SX, LX, LK, QX, QK, U, V, GA, GS, GD, GC, M1, G1, M2, G2, M3, G3,
        load_sem, h_send, h_recv, q_send, q_recv,
        s1, r1, s2, r2, s3, r3, chain,
    ):
        d = lax.axis_index("down")
        c = lax.axis_index("cross")
        core = lax.rem(d, 2)
        chip = lax.div(d, 2)
        z = lax.rem(chip, nz)
        y = lax.div(chip, nz)

        loads = [
            pltpu.make_async_copy(kappa_hbm, E.at[3:11, 0:32, :], load_sem.at[0]),
            pltpu.make_async_copy(mask_hbm, MK, load_sem.at[1]),
            pltpu.make_async_copy(rhs_hbm, R.at[3:11, 0:32, :], load_sem.at[2]),
        ]
        for load in loads:
            load.start()

        d_next, d_prev = lax.rem(d + 1, n_down), lax.rem(d + n_down - 1, n_down)
        c_next, c_prev = lax.rem(c + 1, n_cross), lax.rem(c + n_cross - 1, n_cross)
        near = [(d_prev, c), (d_next, c), (d, c_prev), (d, c_next)]
        corners = [
            (d_prev if sx < 0 else d_next, c_prev if sy < 0 else c_next) for sx, sy in CORNERS
        ]
        n1 = 2 * n_cross
        me1 = c * 2 + core
        group1 = []
        for k in range(1, n1):
            g = lax.rem(me1 + k, n1)
            group1.append((chip * 2 + lax.rem(g, 2), lax.div(g, 2)))
        group2 = [((lax.rem(y + k, ny) * nz + z) * 2 + core, c) for k in range(1, ny)]
        group3 = [((y * nz + lax.rem(z + k, nz)) * 2 + core, c) for k in range(1, nz)]

        barrier = pltpu.get_barrier_semaphore()
        def at_z(by):
            return ((y * nz + lax.rem(z + nz + by, nz)) * 2 + core, c)

        def at_y(by):
            return ((lax.rem(y + ny + by, ny) * nz + z) * 2 + core, c)

        beside = [at_z(1), at_z(-1), at_y(1), at_y(-1)]
        rounds = [beside, [at_z(2), at_z(-2), at_y(2), at_y(-2)], [at_z(2), at_z(-2)]]
        peers = near + corners + group1 + beside
        for peer in peers:
            pl.semaphore_signal(barrier, inc=1, device_id=peer, device_id_type=MESH)

        m_up, m_dn = flag(d > 0), flag(d < n_down - 1)
        m_l, m_r = flag(c > 0), flag(c < n_cross - 1)

        zero8 = jnp.zeros((8, 256), F32)
        for i in (0, 13):
            E[i, 32:40, :] = zero8
        loads[0].wait()
        loads[1].wait()

        @pl.loop(0, 8)
        def _(x):
            kap = E[x + 3, 0:32, :]
            E[x + 3, 0:32, :] = jnp.where(MK[x] > 0, kap * 0.25, kap)

        loads[2].wait()
        sub8 = iota((8, 256), 0)

        @pl.loop(0, 8)
        def _(x):
            SX[0, x] = jnp.where(sub8 < 3, E[x + 3, 0:8, :], pltpu.roll(R[x + 3, 0:8, :], 3, 0))
            SX[1, x] = jnp.where(sub8 >= 5, E[x + 3, 24:32, :], pltpu.roll(R[x + 3, 24:32, :], 5, 0))

        pl.semaphore_wait(barrier, len(peers))

        def announce(k):
            for peer in rounds[k]:
                pl.semaphore_signal(chain.at[k], inc=1, device_id=peer, device_id_type=MESH)

        def heard(k):
            pl.semaphore_wait(chain.at[k], len(rounds[k]))

        def remote(src, dst, send, recv, k, peer):
            return pltpu.make_async_remote_copy(
                src_ref=src, dst_ref=dst, send_sem=send.at[k], recv_sem=recv.at[k],
                device_id=peer, device_id_type=MESH,
            )

        halo = [
            remote(E.at[3:6, 0:32, :], E.at[11:14, 0:32, :], h_send, h_recv, 0, near[0]),
            remote(E.at[8:11, 0:32, :], E.at[0:3, 0:32, :], h_send, h_recv, 1, near[1]),
            remote(SX.at[0], LX.at[1], h_send, h_recv, 2, near[2]),
            remote(SX.at[1], LX.at[0], h_send, h_recv, 3, near[3]),
            remote(R.at[3:5, 0:32, :], R.at[11:13, 0:32, :], h_send, h_recv, 4, near[0]),
            remote(R.at[9:11, 0:32, :], R.at[1:3, 0:32, :], h_send, h_recv, 5, near[1]),
        ]
        for k, (sx, sy) in enumerate(CORNERS):
            rows = slice(0, 2) if sx < 0 else slice(6, 8)
            src = SX.at[0 if sy < 0 else 1, rows]
            halo.append(remote(src, LK.at[3 - k], h_send, h_recv, 6 + k, corners[k]))
        for k in (6, 7, 8, 9, 0, 1, 2, 3, 4, 5):
            halo[k].start()
        announce(0)
        for copy in halo:
            copy.wait_recv()

        def unpack(left, right, i, keep):
            right, left = right * (m_r * keep), left * (m_l * keep)
            E[i, 32:40, :] = jnp.where(sub8 < 3, right, jnp.where(sub8 >= 5, left, 0.0))
            right, left = pltpu.roll(right, 5, 0), pltpu.roll(left, 3, 0)
            R[i, 32:40, :] = jnp.where(sub8 < 2, right, jnp.where(sub8 >= 6, left, 0.0))

        @pl.loop(0, 8)
        def _(x):
            unpack(LX[0, x], LX[1, x], x + 3, 1.0)

        @pl.loop(0, 2)
        def _(x):
            unpack(LK[0, x], LK[1, x], x + 1, m_up)
            unpack(LK[2, x], LK[3, x], x + 11, m_dn)
            R[x + 1, 0:32, :] = R[x + 1, 0:32, :] * m_up
            R[x + 11, 0:32, :] = R[x + 11, 0:32, :] * m_dn

        @pl.loop(0, 3)
        def _(x):
            E[x, 0:32, :] = E[x, 0:32, :] * m_up
            E[x + 11, 0:32, :] = E[x + 11, 0:32, :] * m_dn

        lane40 = iota((40, 256), 1)

        @pl.loop(1, 13)
        def _(i):
            q = E[i]
            back, ahead_, below, above = shifted(q, 1)
            up, dn = E[i - 1], E[i + 1]
            diag = 3.0 * q + 0.5 * (((up + dn) + (back + ahead_)) + (below + above))
            inside = q > 0
            w = jnp.where(inside, OMEGA / jnp.where(inside, diag, 1.0), 0.0)
            FX[i] = 0.5 * (up + q)
            FX[i + 1] = 0.5 * (dn + q)
            FY[0, i] = 0.5 * (back + q)
            FY[1, i] = 0.5 * (ahead_ + q)
            FZ[0, i] = jnp.where(lane40 > 0, 0.5 * (below + q), 0.0)
            FZ[1, i] = jnp.where(lane40 < 255, 0.5 * (above + q), 0.0)
            D[i] = diag
            W[i] = w
            PA[i] = w * R[i]

        heard(0)
        announce(1)

        def coupling(p, i, n):
            back, ahead_, below, above = rolled(p[i], 1, n)
            along = FX[i, :n] * p[i - 1, :n] + FX[i + 1, :n] * p[i + 1, :n]
            across = FY[0, i, :n] * back + FY[1, i, :n] * ahead_
            return (along + across) + (FZ[0, i, :n] * below + FZ[1, i, :n] * above)

        def spread(p, i, n):
            return (1.0 - OMEGA) * p[i, :n] + W[i, :n] * coupling(p, i, n)

        def relax(p, i, n):
            return (1.0 - OMEGA) * p[i, :n] + W[i, :n] * (R[i, :n] + coupling(p, i, n))

        @pl.loop(2, 12)
        def _(i):
            PB[i] = relax(PA, i, 40)

        def residual_row(x, carry):
            acc, con = carry
            i = x + 3
            res = R[i, :32] - D[i, :32] * PB[i, :32] + coupling(PB, i, 32)
            RES[x] = res
            return acc + res, con + E[i]

        acc, con = lax.fori_loop(
            0, 8, residual_row, (jnp.zeros((32, 256), F32), jnp.zeros((40, 256), F32))
        )

        sub40 = iota((40, 256), 0)
        own = sub40 < 32
        down = E[9] + E[10] + E[11] + E[12]
        up = E[1] + E[2] + E[3] + E[4]
        cross = jnp.where((sub40 >= 30) & (sub40 < 34), con, 0.0)
        back = jnp.where((sub40 < 2) | (sub40 >= 38), con, 0.0)
        ends = jnp.where(own & ((lane40 < 2) | (lane40 >= 254)), con, 0.0)
        down = jnp.where(own, down, 0.0)
        outflow = 0.25 * total_of(down + jnp.where(own, up, 0.0) + cross + back + ends)
        sums = [total_of(acc), outflow, 0.25 * total_of(down), 0.25 * total_of(cross)]
        my_lane = lax.rem(z, 2) * 64 + y * 8 + me1
        here = iota((1, 128), 1) == my_lane
        for k, value in enumerate(sums):
            M1[k : k + 1, :] = jnp.where(here, value, 0.0)

        gather1 = [remote(M1, G1.at[k], s1, r1, k, group1[k]) for k in range(n1 - 1)]
        gather2 = [remote(M2, G2.at[k], s2, r2, k, group2[k]) for k in range(ny - 1)]
        gather3 = [remote(M3, G3.at[k], s3, r3, k, group3[k]) for k in range(nz - 1)]
        for copy in gather1:
            copy.start()
        heard(1)
        announce(2)

        zero32 = jnp.zeros((32, 256), F32)
        for ref in (CC, FA, FB):
            ref[0] = zero32
            ref[5] = zero32

        @pl.loop(0, 4)
        def _(x):
            CR[x] = pair_sum(RES[2 * x] + RES[2 * x + 1])
            CC[x + 1] = 0.125 * pair_sum(E[2 * x + 3, 0:32, :] + E[2 * x + 4, 0:32, :])

        lane32, row32 = iota((32, 256), 1), iota((32, 256), 0) % 8

        @pl.loop(1, 5)
        def _(i):
            q = CC[i]
            back, ahead_, below, above = shifted(q, 2, 8)
            up, dn = CC[i - 1], CC[i + 1]
            diag = 12.0 * q + 2.0 * (((up + dn) + (back + ahead_)) + (below + above))
            wt = OMEGA / diag
            TX[i] = 2.0 * (up + q)
            TX[i + 1] = 2.0 * (dn + q)
            TY[0, i] = jnp.where(row32 >= 2, 2.0 * (back + q), 0.0)
            TY[1, i] = jnp.where(row32 < 6, 2.0 * (ahead_ + q), 0.0)
            TZ[0, i] = jnp.where(lane32 >= 2, 2.0 * (below + q), 0.0)
            TZ[1, i] = jnp.where(lane32 < 254, 2.0 * (above + q), 0.0)
            WT[i] = wt
            FA[i] = wt * CR[i - 1]

        def tile_relax(f, i):
            v = f[i]
            back, ahead_, below, above = rolled(v, 2, 32)
            along = TX[i] * f[i - 1] + TX[i + 1] * f[i + 1]
            across = TY[0, i] * back + TY[1, i] * ahead_
            around = (along + across) + (TZ[0, i] * below + TZ[1, i] * above)
            return (1.0 - OMEGA) * v + WT[i] * (CR[i - 1] + around)

        f, g = FA, FB
        for sweep in range(BLOCK_SWEEPS - 1):

            @pl.loop(1, 5)
            def _(i, f=f, g=g):
                g[i] = tile_relax(f, i)

            f, g = g, f

        tile_of_row = iota((32, 256), 0) // 8
        cloud = jnp.zeros((32, 256), F32)
        for t in range(4):
            cloud = jnp.where(tile_of_row == t, flag(route[0, t] >= 0), cloud)

        @pl.loop(0, 4)
        def _(x):
            fix = f[x + 1] * cloud
            Q[2 * x + 3, 0:32, :] = PB[2 * x + 3, 0:32, :] + fix
            Q[2 * x + 4, 0:32, :] = PB[2 * x + 4, 0:32, :] + fix

        for copy in gather1:
            copy.wait_recv()
        row = M1[...]
        for k in range(n1 - 1):
            row = row + G1[k]
        M2[...] = row
        for copy in gather2:
            copy.start()

        src_rows = {-1: slice(3, 5), 1: slice(9, 11)}
        dst_rows = {-1: slice(11, 13), 1: slice(1, 3)}
        src_cols = {-1: slice(0, 8), 1: slice(24, 32)}
        mid, band = slice(3, 11), slice(0, 32)
        fix_halo = []
        for k, sx in enumerate((-1, 1)):
            src, dst = Q.at[src_rows[sx], band, :], Q.at[dst_rows[sx], band, :]
            fix_halo.append(remote(src, dst, q_send, q_recv, k, near[k]))
        for k, sy in enumerate((-1, 1)):
            src = Q.at[mid, src_cols[sy], :]
            fix_halo.append(remote(src, QX.at[1 - k], q_send, q_recv, 2 + k, near[2 + k]))
        for k, (sx, sy) in enumerate(CORNERS):
            src = Q.at[3 if sx < 0 else 10, src_cols[sy], :]
            fix_halo.append(remote(src, QK.at[3 - k], q_send, q_recv, 4 + k, corners[k]))
        for copy in fix_halo:
            copy.start()

        zero32 = jnp.zeros((32, 256), F32)
        zero40 = jnp.zeros((40, 256), F32)
        side = jnp.where(sub8 < 4, m_r, m_l) + zero8

        def ones(i, band_value, tile_value):
            U[i, 0:32, :] = zero32 + band_value
            U[i, 32:40, :] = side * tile_value

        def set_ones(inner, inner_side, outer, outer_side):
            for i, keep in ((1, m_up), (2, m_up), (11, m_dn), (12, m_dn)):
                ones(i, outer * keep, outer_side * keep)

            @pl.loop(3, 11)
            def _(i):
                ones(i, inner, inner_side)

        for target, inner, outer in ((GA, 1.0, 1.0), (GS, 0.0, 0.0)):
            set_ones(inner, 1.0, outer, outer)

            @pl.loop(2, 12)
            def _(i):
                V[i] = spread(U, i, 40)

            @pl.loop(3, 11)
            def _(i, target=target):
                target[i - 3] = spread(V, i, 32)

        for i in (4, 5, 8, 9):
            V[i] = zero40
        for target, outer, rows in ((GD, 1.0, (3, 4, 9, 10)), (GC, 0.0, (3, 10))):
            set_ones(0.0, 0.0, outer, 1.0 - outer)
            for i in (2, 3, 10, 11):
                V[i] = spread(U, i, 40)
            for k, i in enumerate(rows):
                target[k] = spread(V, i, 32)

        for copy in gather2:
            copy.wait_recv()
        row = M2[...]
        for k in range(ny - 1):
            row = row + G2[k]
        M3[...] = row
        heard(2)
        for copy in gather3:
            copy.start()
        for copy in fix_halo:
            copy.wait_recv()

        for lo, hi, keep in ((1, 3, m_up), (3, 11, 1.0), (11, 13, m_dn)):

            @pl.loop(lo, hi)
            def _(i, keep=keep):
                PA[i, 0:32, :] = Q[i, 0:32, :] * keep

        def beside_tile(left, right, keep):
            return jnp.where(sub8 < 4, right * m_r, left * m_l) * keep

        @pl.loop(0, 8)
        def _(x):
            PA[x + 3, 32:40, :] = beside_tile(QX[0, x], QX[1, x], 1.0)

        PA[1, 32:40, :] = zero8
        PA[2, 32:40, :] = beside_tile(QK[0], QK[1], m_up)
        PA[11, 32:40, :] = beside_tile(QK[2], QK[3], m_dn)
        PA[12, 32:40, :] = zero8

        @pl.loop(2, 12)
        def _(i):
            PB[i] = relax(PA, i, 40)

        @pl.loop(3, 11)
        def _(i):
            out[i - 3] = relax(PB, i, 32)

        sub, lane = iota((8, 128), 0), iota((8, 128), 1)
        tz = 2 * sub + lane // 64
        ty = (lane % 64) // 8
        tc = (lane % 8) // 2
        odd = lane % 2 == 1

        for copy in gather3:
            copy.wait_recv()
        table = [jnp.where(sub == lax.div(z, 2), M3[k : k + 1, :], 0.0) for k in range(4)]
        for j in range(nz - 1):
            from_z = lax.rem(z + nz - 1 - j, nz)
            at = sub == lax.div(from_z, 2)
            for k in range(4):
                table[k] = table[k] + jnp.where(at, G3[j, k : k + 1, :], 0.0)
        totals, outs, link_dn, link_cr = table

        def ahead(value, by):
            return pltpu.roll(value, (-by) % 128, 1)

        def shift_rows(value, by):
            return pltpu.roll(value, by % 8, 0)

        def next_parts(value):
            v63 = ahead(value, 63)
            return ahead(value, 1), v63, shift_rows(v63, -1), shift_rows(ahead(value, 71), half - 1)

        def prev_parts(value):
            v63 = ahead(value, -63)
            return (
                ahead(value, -1), v63, shift_rows(v63, 1), shift_rows(ahead(value, -71), 1 - half)
            )

        last = (ty == ny - 1) & (tz == nz - 1)
        first = (ty == 0) & (tz == 0)
        next_at = (
            ~odd,
            odd & (tz % 2 == 0),
            odd & (tz % 2 == 1) & (tz < nz - 1),
            odd & (tz == nz - 1) & ~last,
        )
        prev_at = (
            odd,
            ~odd & (tz % 2 == 1),
            ~odd & (tz % 2 == 0) & (tz > 0),
            ~odd & (tz == 0) & ~first,
        )
        link_up = jnp.zeros((8, 128), F32)
        held = (tz < nz) & (ty < ny) & (tc < n_cross)
        for at, part in zip(prev_at, prev_parts(link_dn)):
            link_up = jnp.where(at & held, part, link_up)
        link_bk = jnp.where((tc > 0) & held, ahead(link_cr, -2), 0.0)
        link_cr = jnp.where(tc < n_cross - 1, link_cr, 0.0)
        next_w = [jnp.where(at, link_dn, 0.0) for at in next_at]
        prev_w = [jnp.where(at, link_up, 0.0) for at in prev_at]

        def operate(value):
            image = outs * value - link_cr * ahead(value, 2) - link_bk * ahead(value, -2)
            for weight, part in zip(next_w, next_parts(value)):
                image = image - weight * part
            for weight, part in zip(prev_w, prev_parts(value)):
                image = image - weight * part
            return image

        def iterate(step, carry):
            answer, resid, search, image, over_norm, over_alpha = carry
            shown = operate(resid)
            norm = total_of(resid * resid)
            weight = total_of(resid * shown)
            beta = norm * over_norm
            alpha = norm / (weight - beta * (norm * over_alpha))
            search = resid + beta * search
            image = shown + beta * image
            answer = answer + alpha * search
            resid = resid - alpha * image
            return answer, resid, search, image, 1.0 / norm, 1.0 / alpha

        none, nil = jnp.zeros((8, 128), F32), jnp.zeros((1, 1), F32)
        start = (none, totals, none, none, nil, nil)
        answer = lax.fori_loop(0, COARSE_ITERS, iterate, start)[0]

        def brick(dd, cc):
            core_b, chip_b = lax.rem(dd, 2), lax.div(dd, 2)
            z_b, y_b = lax.rem(chip_b, nz), lax.div(chip_b, nz)
            at_lane = lax.rem(z_b, 2) * 64 + y_b * 8 + cc * 2 + core_b
            return total_of(jnp.where((sub == lax.div(z_b, 2)) & (lane == at_lane), answer, 0.0))

        mine = brick(d, c)
        near_by = [brick(dd, cc) - mine for dd, cc in near]
        at_corner = [brick(dd, cc) - mine for dd, cc in corners]
        first_half = iota((32, 256), 0) < 16
        beside_by = jnp.where(first_half, near_by[2], near_by[3])

        @pl.loop(0, 8)
        def _(x):
            out[x] = out[x] + (mine * GA[x] + beside_by * GS[x])

        for k, x in enumerate((0, 1, 6, 7)):
            out[x] = out[x] + near_by[k // 2] * GD[k]
        for k, x in enumerate((0, 7)):
            out[x] = out[x] + jnp.where(first_half, at_corner[2 * k], at_corner[2 * k + 1]) * GC[k]

        for copy in halo + gather1 + gather2 + gather3 + fix_halo:
            copy.wait_send()

    return kernel


def solution(mesh):
    n_down, n_cross = mesh.shape["down"], mesh.shape["cross"]
    nz = CHIPS_Z
    ny = n_down // (2 * nz)
    n1 = 2 * n_cross
    big = pltpu.VMEM((14, 40, 256), F32)
    two = pltpu.VMEM((2, 14, 40, 256), F32)
    coarse = pltpu.VMEM((6, 32, 256), F32)
    coarse2 = pltpu.VMEM((2, 6, 32, 256), F32)
    dma = pltpu.SemaphoreType.DMA
    msg = pltpu.VMEM((4, 128), F32)

    def body(right_side, kappa, band_mask, tile_route):
        return pl.pallas_call(
            make_kernel(n_down, n_cross, nz),
            out_shape=pltpu.VMEM(right_side.shape, F32),
            in_specs=[pl.BlockSpec(memory_space=pl.ANY)] * 3
            + [pl.BlockSpec(memory_space=pltpu.SMEM)],
            out_specs=pl.BlockSpec(memory_space=pltpu.VMEM),
            scratch_shapes=[
                big, big, pltpu.VMEM((8, 32, 256), jnp.int32), big, big, big, big, big,
                big, two, two,
                pltpu.VMEM((8, 32, 256), F32),
                pltpu.VMEM((4, 32, 256), F32), coarse, coarse, coarse, coarse2, coarse2,
                coarse, coarse,
                pltpu.VMEM((2, 8, 8, 256), F32), pltpu.VMEM((2, 8, 8, 256), F32),
                pltpu.VMEM((4, 2, 8, 256), F32),
                pltpu.VMEM((2, 8, 8, 256), F32), pltpu.VMEM((4, 8, 256), F32),
                big, big, pltpu.VMEM((8, 32, 256), F32), pltpu.VMEM((8, 32, 256), F32),
                pltpu.VMEM((4, 32, 256), F32), pltpu.VMEM((2, 32, 256), F32),
                msg, pltpu.VMEM((n1 - 1, 4, 128), F32),
                msg, pltpu.VMEM((ny - 1, 4, 128), F32),
                msg, pltpu.VMEM((nz - 1, 4, 128), F32),
                dma((3,)), dma((10,)), dma((10,)), dma((8,)), dma((8,)),
                dma((n1 - 1,)), dma((n1 - 1,)), dma((ny - 1,)), dma((ny - 1,)),
                dma((nz - 1,)), dma((nz - 1,)), pltpu.SemaphoreType.REGULAR((3,)),
            ],
            compiler_params=pltpu.CompilerParams(collective_id=0, has_side_effects=True),
            name="cycle",
        )(right_side, kappa, band_mask, tile_route)

    return jax.shard_map(
        body,
        mesh=mesh,
        in_specs=(
            P("down", "cross", None),
            P("down", "cross", None),
            P("down", "cross", None),
            P("down", "cross"),
        ),
        out_specs=P("down", "cross", None),
        check_vma=False,
    )
```

```python
import jax
import jax.numpy as jnp
from jax import lax
from jax.experimental import pallas as pl
from jax.experimental.pallas import tpu as pltpu
from jax.sharding import PartitionSpec as P

OMEGA = 0.8
BLOCK_SWEEPS = 4
COARSE_ITERS = 12
CHIPS_Z = 12

MESH = pl.DeviceIdType.MESH
CORNERS = ((-1, -1), (-1, 1), (1, -1), (1, 1))
F32 = jnp.float32


def iota(shape, dim):
    return lax.broadcasted_iota(jnp.int32, shape, dim)


def flag(cond):
    return jnp.where(cond, 1.0, 0.0).astype(F32)


def total_of(value):
    return jnp.sum(jnp.sum(value, axis=0, keepdims=True), axis=1, keepdims=True)


def shifted(value, by, tile=0):
    rows, lanes = value.shape
    row, lane = iota(value.shape, 0) % max(tile, 1), iota(value.shape, 1)
    back, ahead = pltpu.roll(value, by, 0), pltpu.roll(value, rows - by, 0)
    if tile:
        back = jnp.where(row >= by, back, 0.0)
        ahead = jnp.where(row < tile - by, ahead, 0.0)
    below = jnp.where(lane >= by, pltpu.roll(value, by, 1), 0.0)
    above = jnp.where(lane < lanes - by, pltpu.roll(value, lanes - by, 1), 0.0)
    return back, ahead, below, above


def rolled(value, by, rows_out):
    rows, lanes = value.shape
    return (
        pltpu.roll(value, by, 0)[:rows_out],
        pltpu.roll(value, rows - by, 0)[:rows_out],
        pltpu.roll(value[:rows_out], by, 1),
        pltpu.roll(value[:rows_out], lanes - by, 1),
    )


def pair_sum(value):
    rows, lanes = value.shape
    row, lane = iota(value.shape, 0), iota(value.shape, 1)
    value = value + jnp.where(row % 2 == 0, pltpu.roll(value, rows - 1, 0), pltpu.roll(value, 1, 0))
    return value + jnp.where(
        lane % 2 == 0, pltpu.roll(value, lanes - 1, 1), pltpu.roll(value, 1, 1)
    )


def make_kernel(n_down, n_cross, nz):
    ny = n_down // (2 * nz)
    half = nz // 2

    def kernel(
        rhs_hbm, kappa_hbm, mask_hbm, route, out,
        E, R, MK, D, W, PA, PB, Q, FX, FY, FZ, RES, CR, CC, WT, TX, TY, TZ, FA, FB,
        SX, LX, LK, QX, QK, U, V, GA, GS, GD, GC, M1, G1, M2, G2, M3, G3,
        load_sem, h_send, h_recv, q_send, q_recv,
        s1, r1, s2, r2, s3, r3, chain,
    ):
        d = lax.axis_index("down")
        c = lax.axis_index("cross")
        core = lax.rem(d, 2)
        chip = lax.div(d, 2)
        z = lax.rem(chip, nz)
        y = lax.div(chip, nz)

        loads = [
            pltpu.make_async_copy(kappa_hbm, E.at[3:11, 0:32, :], load_sem.at[0]),
            pltpu.make_async_copy(mask_hbm, MK, load_sem.at[1]),
            pltpu.make_async_copy(rhs_hbm, R.at[3:11, 0:32, :], load_sem.at[2]),
        ]
        for load in loads:
            load.start()

        d_next, d_prev = lax.rem(d + 1, n_down), lax.rem(d + n_down - 1, n_down)
        c_next, c_prev = lax.rem(c + 1, n_cross), lax.rem(c + n_cross - 1, n_cross)
        near = [(d_prev, c), (d_next, c), (d, c_prev), (d, c_next)]
        corners = [
            (d_prev if sx < 0 else d_next, c_prev if sy < 0 else c_next) for sx, sy in CORNERS
        ]
        n1 = 2 * n_cross
        me1 = c * 2 + core
        group1 = []
        for k in range(1, n1):
            g = lax.rem(me1 + k, n1)
            group1.append((chip * 2 + lax.rem(g, 2), lax.div(g, 2)))
        group2 = [((lax.rem(y + k, ny) * nz + z) * 2 + core, c) for k in range(1, ny)]
        group3 = [((y * nz + lax.rem(z + k, nz)) * 2 + core, c) for k in range(1, nz)]

        barrier = pltpu.get_barrier_semaphore()
        def at_z(by):
            return ((y * nz + lax.rem(z + nz + by, nz)) * 2 + core, c)

        def at_y(by):
            return ((lax.rem(y + ny + by, ny) * nz + z) * 2 + core, c)

        beside = [at_z(1), at_z(-1), at_y(1), at_y(-1)]
        rounds = [beside, [at_z(2), at_z(-2), at_y(2), at_y(-2)], [at_z(2), at_z(-2)]]
        peers = near + corners + group1 + beside
        for peer in peers:
            pl.semaphore_signal(barrier, inc=1, device_id=peer, device_id_type=MESH)

        m_up, m_dn = flag(d > 0), flag(d < n_down - 1)
        m_l, m_r = flag(c > 0), flag(c < n_cross - 1)

        zero8 = jnp.zeros((8, 256), F32)
        for i in (0, 13):
            E[i, 32:40, :] = zero8
        loads[0].wait()
        loads[1].wait()

        @pl.loop(0, 8)
        def _(x):
            kap = E[x + 3, 0:32, :]
            E[x + 3, 0:32, :] = jnp.where(MK[x] > 0, kap * 0.25, kap)

        loads[2].wait()
        sub8 = iota((8, 256), 0)

        @pl.loop(0, 8)
        def _(x):
            SX[0, x] = jnp.where(sub8 < 3, E[x + 3, 0:8, :], pltpu.roll(R[x + 3, 0:8, :], 3, 0))
            SX[1, x] = jnp.where(sub8 >= 5, E[x + 3, 24:32, :], pltpu.roll(R[x + 3, 24:32, :], 5, 0))

        pl.semaphore_wait(barrier, len(peers))

        def announce(k):
            for peer in rounds[k]:
                pl.semaphore_signal(chain.at[k], inc=1, device_id=peer, device_id_type=MESH)

        def heard(k):
            pl.semaphore_wait(chain.at[k], len(rounds[k]))

        def remote(src, dst, send, recv, k, peer):
            return pltpu.make_async_remote_copy(
                src_ref=src, dst_ref=dst, send_sem=send.at[k], recv_sem=recv.at[k],
                device_id=peer, device_id_type=MESH,
            )

        halo = [
            remote(E.at[3:6, 0:32, :], E.at[11:14, 0:32, :], h_send, h_recv, 0, near[0]),
            remote(E.at[8:11, 0:32, :], E.at[0:3, 0:32, :], h_send, h_recv, 1, near[1]),
            remote(SX.at[0], LX.at[1], h_send, h_recv, 2, near[2]),
            remote(SX.at[1], LX.at[0], h_send, h_recv, 3, near[3]),
            remote(R.at[3:5, 0:32, :], R.at[11:13, 0:32, :], h_send, h_recv, 4, near[0]),
            remote(R.at[9:11, 0:32, :], R.at[1:3, 0:32, :], h_send, h_recv, 5, near[1]),
        ]
        for k, (sx, sy) in enumerate(CORNERS):
            rows = slice(0, 2) if sx < 0 else slice(6, 8)
            src = SX.at[0 if sy < 0 else 1, rows]
            halo.append(remote(src, LK.at[3 - k], h_send, h_recv, 6 + k, corners[k]))
        for k in (0, 1, 2, 3, 6, 7, 8, 9, 4, 5):
            halo[k].start()
        announce(0)

        lane32 = iota((32, 256), 1)

        @pl.loop(3, 11)
        def _(i):
            q = E[i, 0:32, :]
            below = jnp.where(lane32 > 0, pltpu.roll(q, 1, 1), 0.0)
            above = jnp.where(lane32 < 255, pltpu.roll(q, 255, 1), 0.0)
            FZ[0, i, 0:32, :] = jnp.where(lane32 > 0, 0.5 * (below + q), 0.0)
            FZ[1, i, 0:32, :] = jnp.where(lane32 < 255, 0.5 * (above + q), 0.0)
            D[i, 0:32, :] = 3.0 * q + 0.5 * (below + above)

        @pl.loop(4, 11)
        def _(i):
            FX[i, 0:32, :] = 0.5 * (E[i - 1, 0:32, :] + E[i, 0:32, :])

        for k in (0, 1, 2, 3, 6, 7, 8, 9):
            halo[k].wait_recv()

        def unpack(left, right, i, keep):
            right, left = right * (m_r * keep), left * (m_l * keep)
            E[i, 32:40, :] = jnp.where(sub8 < 3, right, jnp.where(sub8 >= 5, left, 0.0))
            right, left = pltpu.roll(right, 5, 0), pltpu.roll(left, 3, 0)
            R[i, 32:40, :] = jnp.where(sub8 < 2, right, jnp.where(sub8 >= 6, left, 0.0))

        @pl.loop(0, 8)
        def _(x):
            unpack(LX[0, x], LX[1, x], x + 3, 1.0)

        @pl.loop(0, 2)
        def _(x):
            unpack(LK[0, x], LK[1, x], x + 1, m_up)
            unpack(LK[2, x], LK[3, x], x + 11, m_dn)

        @pl.loop(0, 3)
        def _(x):
            E[x, 0:32, :] = E[x, 0:32, :] * m_up
            E[x + 11, 0:32, :] = E[x + 11, 0:32, :] * m_dn

        lane40, lane8 = iota((40, 256), 1), iota((8, 256), 1)

        def weigh(q, diag):
            inside = q > 0
            return jnp.where(inside, OMEGA / jnp.where(inside, diag, 1.0), 0.0)

        @pl.loop(3, 11)
        def _(i):
            q, up, dn = E[i], E[i - 1], E[i + 1]
            back, ahead_ = pltpu.roll(q, 1, 0), pltpu.roll(q, 39, 0)
            FY[0, i] = 0.5 * (back + q)
            FY[1, i] = 0.5 * (ahead_ + q)
            around = 0.5 * ((up + dn) + (back + ahead_))
            g = q[32:40]
            below = jnp.where(lane8 > 0, pltpu.roll(g, 1, 1), 0.0)
            above = jnp.where(lane8 < 255, pltpu.roll(g, 255, 1), 0.0)
            FZ[0, i, 32:40, :] = jnp.where(lane8 > 0, 0.5 * (below + g), 0.0)
            FZ[1, i, 32:40, :] = jnp.where(lane8 < 255, 0.5 * (above + g), 0.0)
            FX[i, 32:40, :] = 0.5 * (up[32:40] + g)
            diag = D[i, 0:32, :] + around[0:32]
            diag_g = 3.0 * g + 0.5 * (below + above) + around[32:40]
            w, w_g = weigh(q[0:32], diag), weigh(g, diag_g)
            D[i, 0:32, :] = diag
            W[i, 0:32, :] = w
            W[i, 32:40, :] = w_g
            PA[i, 0:32, :] = w * R[i, 0:32, :]
            PA[i, 32:40, :] = w_g * R[i, 32:40, :]

        for k in (4, 5):
            halo[k].wait_recv()

        @pl.loop(0, 2)
        def _(x):
            R[x + 1, 0:32, :] = R[x + 1, 0:32, :] * m_up
            R[x + 11, 0:32, :] = R[x + 11, 0:32, :] * m_dn

        @pl.loop(0, 4)
        def _(x):
            i = x + 1 + 8 * lax.div(x, 2)
            q = E[i]
            back, ahead_, below, above = shifted(q, 1)
            up, dn = E[i - 1], E[i + 1]
            FX[i] = 0.5 * (up + q)
            FY[0, i] = 0.5 * (back + q)
            FY[1, i] = 0.5 * (ahead_ + q)
            FZ[0, i] = jnp.where(lane40 > 0, 0.5 * (below + q), 0.0)
            FZ[1, i] = jnp.where(lane40 < 255, 0.5 * (above + q), 0.0)
            w = weigh(q, 3.0 * q + 0.5 * (((up + dn) + (back + ahead_)) + (below + above)))
            W[i] = w
            PA[i] = w * R[i]

        FX[3, 0:32, :] = 0.5 * (E[2, 0:32, :] + E[3, 0:32, :])

        heard(0)
        announce(1)

        def coupling(p, i, n):
            back, ahead_, below, above = rolled(p[i], 1, n)
            along = FX[i, :n] * p[i - 1, :n] + FX[i + 1, :n] * p[i + 1, :n]
            across = FY[0, i, :n] * back + FY[1, i, :n] * ahead_
            return (along + across) + (FZ[0, i, :n] * below + FZ[1, i, :n] * above)

        def spread(p, i, n):
            return (1.0 - OMEGA) * p[i, :n] + W[i, :n] * coupling(p, i, n)

        def relax(p, i, n):
            return (1.0 - OMEGA) * p[i, :n] + W[i, :n] * (R[i, :n] + coupling(p, i, n))

        @pl.loop(2, 12)
        def _(i):
            PB[i] = relax(PA, i, 40)

        def residual_row(x, carry):
            acc, con = carry
            i = x + 3
            res = R[i, :32] - D[i, :32] * PB[i, :32] + coupling(PB, i, 32)
            RES[x] = res
            return acc + res, con + E[i]

        acc, con = lax.fori_loop(
            0, 8, residual_row, (jnp.zeros((32, 256), F32), jnp.zeros((40, 256), F32))
        )

        sub40 = iota((40, 256), 0)
        own = sub40 < 32
        down = E[9] + E[10] + E[11] + E[12]
        up = E[1] + E[2] + E[3] + E[4]
        cross = jnp.where((sub40 >= 30) & (sub40 < 34), con, 0.0)
        back = jnp.where((sub40 < 2) | (sub40 >= 38), con, 0.0)
        ends = jnp.where(own & ((lane40 < 2) | (lane40 >= 254)), con, 0.0)
        down = jnp.where(own, down, 0.0)
        outflow = 0.25 * total_of(down + jnp.where(own, up, 0.0) + cross + back + ends)
        sums = [total_of(acc), outflow, 0.25 * total_of(down), 0.25 * total_of(cross)]
        my_lane = lax.rem(z, 2) * 64 + y * 8 + me1
        here = iota((1, 128), 1) == my_lane
        for k, value in enumerate(sums):
            M1[k : k + 1, :] = jnp.where(here, value, 0.0)

        gather1 = [remote(M1, G1.at[k], s1, r1, k, group1[k]) for k in range(n1 - 1)]
        gather2 = [remote(M2, G2.at[k], s2, r2, k, group2[k]) for k in range(ny - 1)]
        gather3 = [remote(M3, G3.at[k], s3, r3, k, group3[k]) for k in range(nz - 1)]

        def launch(copies):
            middle = (len(copies) - 1) / 2
            for k in sorted(range(len(copies)), key=lambda k: abs(k - middle)):
                copies[k].start()

        launch(gather1)
        heard(1)
        announce(2)

        zero32 = jnp.zeros((32, 256), F32)
        for ref in (CC, FA, FB):
            ref[0] = zero32
            ref[5] = zero32

        @pl.loop(0, 4)
        def _(x):
            CR[x] = pair_sum(RES[2 * x] + RES[2 * x + 1])
            CC[x + 1] = 0.125 * pair_sum(E[2 * x + 3, 0:32, :] + E[2 * x + 4, 0:32, :])

        row32 = iota((32, 256), 0) % 8

        @pl.loop(1, 5)
        def _(i):
            q = CC[i]
            back, ahead_, below, above = shifted(q, 2, 8)
            up, dn = CC[i - 1], CC[i + 1]
            diag = 12.0 * q + 2.0 * (((up + dn) + (back + ahead_)) + (below + above))
            wt = OMEGA / diag
            TX[i] = 2.0 * (up + q)
            TX[i + 1] = 2.0 * (dn + q)
            TY[0, i] = jnp.where(row32 >= 2, 2.0 * (back + q), 0.0)
            TY[1, i] = jnp.where(row32 < 6, 2.0 * (ahead_ + q), 0.0)
            TZ[0, i] = jnp.where(lane32 >= 2, 2.0 * (below + q), 0.0)
            TZ[1, i] = jnp.where(lane32 < 254, 2.0 * (above + q), 0.0)
            WT[i] = wt
            FA[i] = wt * CR[i - 1]

        def tile_relax(f, i):
            v = f[i]
            back, ahead_, below, above = rolled(v, 2, 32)
            along = TX[i] * f[i - 1] + TX[i + 1] * f[i + 1]
            across = TY[0, i] * back + TY[1, i] * ahead_
            around = (along + across) + (TZ[0, i] * below + TZ[1, i] * above)
            return (1.0 - OMEGA) * v + WT[i] * (CR[i - 1] + around)

        f, g = FA, FB
        for sweep in range(BLOCK_SWEEPS - 1):

            @pl.loop(1, 5)
            def _(i, f=f, g=g):
                g[i] = tile_relax(f, i)

            f, g = g, f

        tile_of_row = iota((32, 256), 0) // 8
        cloud = jnp.zeros((32, 256), F32)
        for t in range(4):
            cloud = jnp.where(tile_of_row == t, flag(route[0, t] >= 0), cloud)

        @pl.loop(0, 4)
        def _(x):
            fix = f[x + 1] * cloud
            Q[2 * x + 3, 0:32, :] = PB[2 * x + 3, 0:32, :] + fix
            Q[2 * x + 4, 0:32, :] = PB[2 * x + 4, 0:32, :] + fix

        for copy in gather1:
            copy.wait_recv()
        row = M1[...]
        for k in range(n1 - 1):
            row = row + G1[k]
        M2[...] = row
        launch(gather2)

        src_rows = {-1: slice(3, 5), 1: slice(9, 11)}
        dst_rows = {-1: slice(11, 13), 1: slice(1, 3)}
        src_cols = {-1: slice(0, 8), 1: slice(24, 32)}
        mid, band = slice(3, 11), slice(0, 32)
        fix_halo = []
        for k, sx in enumerate((-1, 1)):
            src, dst = Q.at[src_rows[sx], band, :], Q.at[dst_rows[sx], band, :]
            fix_halo.append(remote(src, dst, q_send, q_recv, k, near[k]))
        for k, sy in enumerate((-1, 1)):
            src = Q.at[mid, src_cols[sy], :]
            fix_halo.append(remote(src, QX.at[1 - k], q_send, q_recv, 2 + k, near[2 + k]))
        for k, (sx, sy) in enumerate(CORNERS):
            src = Q.at[3 if sx < 0 else 10, src_cols[sy], :]
            fix_halo.append(remote(src, QK.at[3 - k], q_send, q_recv, 4 + k, corners[k]))
        for copy in fix_halo:
            copy.start()

        zero32 = jnp.zeros((32, 256), F32)
        zero40 = jnp.zeros((40, 256), F32)
        side = jnp.where(sub8 < 4, m_r, m_l) + zero8

        def ones(i, band_value, tile_value):
            U[i, 0:32, :] = zero32 + band_value
            U[i, 32:40, :] = side * tile_value

        def set_ones(inner, inner_side, outer, outer_side):
            for i, keep in ((1, m_up), (2, m_up), (11, m_dn), (12, m_dn)):
                ones(i, outer * keep, outer_side * keep)

            @pl.loop(3, 11)
            def _(i):
                ones(i, inner, inner_side)

        for target, inner, outer in ((GA, 1.0, 1.0), (GS, 0.0, 0.0)):
            set_ones(inner, 1.0, outer, outer)

            @pl.loop(2, 12)
            def _(i):
                V[i] = spread(U, i, 40)

            @pl.loop(3, 11)
            def _(i, target=target):
                target[i - 3] = spread(V, i, 32)

        for i in (4, 5, 8, 9):
            V[i] = zero40
        for target, outer, rows in ((GD, 1.0, (3, 4, 9, 10)), (GC, 0.0, (3, 10))):
            set_ones(0.0, 0.0, outer, 1.0 - outer)
            for i in (2, 3, 10, 11):
                V[i] = spread(U, i, 40)
            for k, i in enumerate(rows):
                target[k] = spread(V, i, 32)

        for copy in gather2:
            copy.wait_recv()
        row = M2[...]
        for k in range(ny - 1):
            row = row + G2[k]
        M3[...] = row
        heard(2)
        launch(gather3)
        for copy in fix_halo:
            copy.wait_recv()

        for lo, hi, keep in ((1, 3, m_up), (3, 11, 1.0), (11, 13, m_dn)):

            @pl.loop(lo, hi)
            def _(i, keep=keep):
                PA[i, 0:32, :] = Q[i, 0:32, :] * keep

        def beside_tile(left, right, keep):
            return jnp.where(sub8 < 4, right * m_r, left * m_l) * keep

        @pl.loop(0, 8)
        def _(x):
            PA[x + 3, 32:40, :] = beside_tile(QX[0, x], QX[1, x], 1.0)

        PA[1, 32:40, :] = zero8
        PA[2, 32:40, :] = beside_tile(QK[0], QK[1], m_up)
        PA[11, 32:40, :] = beside_tile(QK[2], QK[3], m_dn)
        PA[12, 32:40, :] = zero8

        @pl.loop(2, 12)
        def _(i):
            PB[i] = relax(PA, i, 40)

        @pl.loop(3, 11)
        def _(i):
            out[i - 3] = relax(PB, i, 32)

        sub, lane = iota((8, 128), 0), iota((8, 128), 1)
        tz = 2 * sub + lane // 64
        ty = (lane % 64) // 8
        tc = (lane % 8) // 2
        odd = lane % 2 == 1

        for copy in halo + gather1 + gather2 + fix_halo + gather3:
            copy.wait_send()
        for copy in gather3:
            copy.wait_recv()
        table = [jnp.where(sub == lax.div(z, 2), M3[k : k + 1, :], 0.0) for k in range(4)]
        for j in range(nz - 1):
            from_z = lax.rem(z + nz - 1 - j, nz)
            at = sub == lax.div(from_z, 2)
            for k in range(4):
                table[k] = table[k] + jnp.where(at, G3[j, k : k + 1, :], 0.0)
        totals, outs, link_dn, link_cr = table

        def ahead(value, by):
            return pltpu.roll(value, (-by) % 128, 1)

        def shift_rows(value, by):
            return pltpu.roll(value, by % 8, 0)

        def next_parts(value):
            v63 = ahead(value, 63)
            return ahead(value, 1), v63, shift_rows(v63, -1), shift_rows(ahead(value, 71), half - 1)

        def prev_parts(value):
            v63 = ahead(value, -63)
            return (
                ahead(value, -1), v63, shift_rows(v63, 1), shift_rows(ahead(value, -71), 1 - half)
            )

        last = (ty == ny - 1) & (tz == nz - 1)
        first = (ty == 0) & (tz == 0)
        next_at = (
            ~odd,
            odd & (tz % 2 == 0),
            odd & (tz % 2 == 1) & (tz < nz - 1),
            odd & (tz == nz - 1) & ~last,
        )
        prev_at = (
            odd,
            ~odd & (tz % 2 == 1),
            ~odd & (tz % 2 == 0) & (tz > 0),
            ~odd & (tz == 0) & ~first,
        )
        link_up = jnp.zeros((8, 128), F32)
        held = (tz < nz) & (ty < ny) & (tc < n_cross)
        for at, part in zip(prev_at, prev_parts(link_dn)):
            link_up = jnp.where(at & held, part, link_up)
        link_bk = jnp.where((tc > 0) & held, ahead(link_cr, -2), 0.0)
        link_cr = jnp.where(tc < n_cross - 1, link_cr, 0.0)
        next_w = [jnp.where(at, link_dn, 0.0) for at in next_at]
        prev_w = [jnp.where(at, link_up, 0.0) for at in prev_at]

        def operate(value):
            image = outs * value - link_cr * ahead(value, 2) - link_bk * ahead(value, -2)
            for weight, part in zip(next_w, next_parts(value)):
                image = image - weight * part
            for weight, part in zip(prev_w, prev_parts(value)):
                image = image - weight * part
            return image

        def iterate(step, carry):
            answer, resid, search, image, over_norm, over_alpha = carry
            shown = operate(resid)
            norm = total_of(resid * resid)
            weight = total_of(resid * shown)
            beta = norm * over_norm
            alpha = norm / (weight - beta * (norm * over_alpha))
            search = resid + beta * search
            image = shown + beta * image
            answer = answer + alpha * search
            resid = resid - alpha * image
            return answer, resid, search, image, 1.0 / norm, 1.0 / alpha

        none, nil = jnp.zeros((8, 128), F32), jnp.zeros((1, 1), F32)
        start = (none, totals, none, none, nil, nil)
        answer = lax.fori_loop(0, COARSE_ITERS, iterate, start)[0]

        def brick(dd, cc):
            core_b, chip_b = lax.rem(dd, 2), lax.div(dd, 2)
            z_b, y_b = lax.rem(chip_b, nz), lax.div(chip_b, nz)
            at_lane = lax.rem(z_b, 2) * 64 + y_b * 8 + cc * 2 + core_b
            return total_of(jnp.where((sub == lax.div(z_b, 2)) & (lane == at_lane), answer, 0.0))

        mine = brick(d, c)
        near_by = [brick(dd, cc) - mine for dd, cc in near]
        at_corner = [brick(dd, cc) - mine for dd, cc in corners]
        first_half = iota((32, 256), 0) < 16
        beside_by = jnp.where(first_half, near_by[2], near_by[3])

        @pl.loop(0, 8)
        def _(x):
            out[x] = out[x] + (mine * GA[x] + beside_by * GS[x])

        for k, x in enumerate((0, 1, 6, 7)):
            out[x] = out[x] + near_by[k // 2] * GD[k]
        for k, x in enumerate((0, 7)):
            out[x] = out[x] + jnp.where(first_half, at_corner[2 * k], at_corner[2 * k + 1]) * GC[k]


    return kernel


def solution(mesh):
    n_down, n_cross = mesh.shape["down"], mesh.shape["cross"]
    nz = CHIPS_Z
    ny = n_down // (2 * nz)
    n1 = 2 * n_cross
    big = pltpu.VMEM((14, 40, 256), F32)
    two = pltpu.VMEM((2, 14, 40, 256), F32)
    coarse = pltpu.VMEM((6, 32, 256), F32)
    coarse2 = pltpu.VMEM((2, 6, 32, 256), F32)
    dma = pltpu.SemaphoreType.DMA
    msg = pltpu.VMEM((4, 128), F32)

    def body(right_side, kappa, band_mask, tile_route):
        return pl.pallas_call(
            make_kernel(n_down, n_cross, nz),
            out_shape=pltpu.VMEM(right_side.shape, F32),
            in_specs=[pl.BlockSpec(memory_space=pl.ANY)] * 3
            + [pl.BlockSpec(memory_space=pltpu.SMEM)],
            out_specs=pl.BlockSpec(memory_space=pltpu.VMEM),
            scratch_shapes=[
                big, big, pltpu.VMEM((8, 32, 256), jnp.int32), big, big, big, big, big,
                big, two, two,
                pltpu.VMEM((8, 32, 256), F32),
                pltpu.VMEM((4, 32, 256), F32), coarse, coarse, coarse, coarse2, coarse2,
                coarse, coarse,
                pltpu.VMEM((2, 8, 8, 256), F32), pltpu.VMEM((2, 8, 8, 256), F32),
                pltpu.VMEM((4, 2, 8, 256), F32),
                pltpu.VMEM((2, 8, 8, 256), F32), pltpu.VMEM((4, 8, 256), F32),
                big, big, pltpu.VMEM((8, 32, 256), F32), pltpu.VMEM((8, 32, 256), F32),
                pltpu.VMEM((4, 32, 256), F32), pltpu.VMEM((2, 32, 256), F32),
                msg, pltpu.VMEM((n1 - 1, 4, 128), F32),
                msg, pltpu.VMEM((ny - 1, 4, 128), F32),
                msg, pltpu.VMEM((nz - 1, 4, 128), F32),
                dma((3,)), dma((10,)), dma((10,)), dma((8,)), dma((8,)),
                dma((n1 - 1,)), dma((n1 - 1,)), dma((ny - 1,)), dma((ny - 1,)),
                dma((nz - 1,)), dma((nz - 1,)), pltpu.SemaphoreType.REGULAR((3,)),
            ],
            compiler_params=pltpu.CompilerParams(collective_id=0, has_side_effects=True),
            name="cycle",
        )(right_side, kappa, band_mask, tile_route)

    return jax.shard_map(
        body,
        mesh=mesh,
        in_specs=(
            P("down", "cross", None),
            P("down", "cross", None),
            P("down", "cross", None),
            P("down", "cross"),
        ),
        out_specs=P("down", "cross", None),
        check_vma=False,
    )
```

```python
import jax
import jax.numpy as jnp
from jax import lax
from jax.experimental import pallas as pl
from jax.experimental.pallas import tpu as pltpu
from jax.sharding import PartitionSpec as P

OMEGA = 0.8
BLOCK_SWEEPS = 4
COARSE_ITERS = 12
CHIPS_Z = 12

MESH = pl.DeviceIdType.MESH
CORNERS = ((-1, -1), (-1, 1), (1, -1), (1, 1))
F32 = jnp.float32


def iota(shape, dim):
    return lax.broadcasted_iota(jnp.int32, shape, dim)


def flag(cond):
    return jnp.where(cond, 1.0, 0.0).astype(F32)


def total_of(value):
    return jnp.sum(jnp.sum(value, axis=0, keepdims=True), axis=1, keepdims=True)


def shifted(value, by, tile=0):
    rows, lanes = value.shape
    row, lane = iota(value.shape, 0) % max(tile, 1), iota(value.shape, 1)
    back, ahead = pltpu.roll(value, by, 0), pltpu.roll(value, rows - by, 0)
    if tile:
        back = jnp.where(row >= by, back, 0.0)
        ahead = jnp.where(row < tile - by, ahead, 0.0)
    below = jnp.where(lane >= by, pltpu.roll(value, by, 1), 0.0)
    above = jnp.where(lane < lanes - by, pltpu.roll(value, lanes - by, 1), 0.0)
    return back, ahead, below, above


def rolled(value, by, rows_out):
    rows, lanes = value.shape
    return (
        pltpu.roll(value, by, 0)[:rows_out],
        pltpu.roll(value, rows - by, 0)[:rows_out],
        pltpu.roll(value[:rows_out], by, 1),
        pltpu.roll(value[:rows_out], lanes - by, 1),
    )


def pair_sum(value):
    rows, lanes = value.shape
    row, lane = iota(value.shape, 0), iota(value.shape, 1)
    value = value + jnp.where(row % 2 == 0, pltpu.roll(value, rows - 1, 0), pltpu.roll(value, 1, 0))
    return value + jnp.where(
        lane % 2 == 0, pltpu.roll(value, lanes - 1, 1), pltpu.roll(value, 1, 1)
    )


def make_kernel(n_down, n_cross, nz):
    ny = n_down // (2 * nz)
    half = nz // 2

    def kernel(
        rhs_hbm, kappa_hbm, mask_hbm, route, out,
        E, R, MK, D, W, PA, PB, Q, FX, FY, FZ, RES, CR, CC, WT, TX, TY, TZ, FA, FB,
        SX, LX, LK, QX, QK, U, V, S, GA, GS, GD, GC, M1, G1, M2, G2, M3, G3,
        load_sem, h_send, h_recv, q_send, q_recv,
        s1, r1, s2, r2, s3, r3, chain,
    ):
        d = lax.axis_index("down")
        c = lax.axis_index("cross")
        core = lax.rem(d, 2)
        chip = lax.div(d, 2)
        z = lax.rem(chip, nz)
        y = lax.div(chip, nz)

        loads = [
            pltpu.make_async_copy(kappa_hbm, E.at[3:11, 0:32, :], load_sem.at[0]),
            pltpu.make_async_copy(mask_hbm, MK, load_sem.at[1]),
            pltpu.make_async_copy(rhs_hbm, R.at[3:11, 0:32, :], load_sem.at[2]),
        ]
        for load in loads:
            load.start()

        d_next, d_prev = lax.rem(d + 1, n_down), lax.rem(d + n_down - 1, n_down)
        c_next, c_prev = lax.rem(c + 1, n_cross), lax.rem(c + n_cross - 1, n_cross)
        near = [(d_prev, c), (d_next, c), (d, c_prev), (d, c_next)]
        corners = [
            (d_prev if sx < 0 else d_next, c_prev if sy < 0 else c_next) for sx, sy in CORNERS
        ]
        n1 = 2 * n_cross
        me1 = c * 2 + core
        group1 = []
        for k in range(1, n1):
            g = lax.rem(me1 + k, n1)
            group1.append((chip * 2 + lax.rem(g, 2), lax.div(g, 2)))
        group2 = [((lax.rem(y + k, ny) * nz + z) * 2 + core, c) for k in range(1, ny)]
        group3 = [((y * nz + lax.rem(z + k, nz)) * 2 + core, c) for k in range(1, nz)]

        barrier = pltpu.get_barrier_semaphore()
        def at_z(by):
            return ((y * nz + lax.rem(z + nz + by, nz)) * 2 + core, c)

        def at_y(by):
            return ((lax.rem(y + ny + by, ny) * nz + z) * 2 + core, c)

        beside = [at_z(1), at_z(-1), at_y(1), at_y(-1)]
        rounds = [beside, [at_z(2), at_z(-2), at_y(2), at_y(-2)], [at_z(2), at_z(-2)]]
        peers = near + corners + group1 + beside
        for peer in peers:
            pl.semaphore_signal(barrier, inc=1, device_id=peer, device_id_type=MESH)

        m_up, m_dn = flag(d > 0), flag(d < n_down - 1)
        m_l, m_r = flag(c > 0), flag(c < n_cross - 1)

        zero8 = jnp.zeros((8, 256), F32)
        for i in (0, 13):
            E[i, 32:40, :] = zero8
        loads[0].wait()
        loads[1].wait()

        @pl.loop(0, 8)
        def _(x):
            kap = E[x + 3, 0:32, :]
            E[x + 3, 0:32, :] = jnp.where(MK[x] > 0, kap * 0.25, kap)

        sub8 = iota((8, 256), 0)

        pl.semaphore_wait(barrier, len(peers))

        def announce(k):
            for peer in rounds[k]:
                pl.semaphore_signal(chain.at[k], inc=1, device_id=peer, device_id_type=MESH)

        def heard(k):
            pl.semaphore_wait(chain.at[k], len(rounds[k]))

        def remote(src, dst, send, recv, k, peer):
            return pltpu.make_async_remote_copy(
                src_ref=src, dst_ref=dst, send_sem=send.at[k], recv_sem=recv.at[k],
                device_id=peer, device_id_type=MESH,
            )

        halo = [
            remote(E.at[3:6, 0:32, :], E.at[11:14, 0:32, :], h_send, h_recv, 0, near[0]),
            remote(E.at[8:11, 0:32, :], E.at[0:3, 0:32, :], h_send, h_recv, 1, near[1]),
            remote(SX.at[0], LX.at[1], h_send, h_recv, 2, near[2]),
            remote(SX.at[1], LX.at[0], h_send, h_recv, 3, near[3]),
            remote(R.at[3:5, 0:32, :], R.at[11:13, 0:32, :], h_send, h_recv, 4, near[0]),
            remote(R.at[9:11, 0:32, :], R.at[1:3, 0:32, :], h_send, h_recv, 5, near[1]),
        ]
        for k, (sx, sy) in enumerate(CORNERS):
            rows = slice(0, 2) if sx < 0 else slice(6, 8)
            src = SX.at[0 if sy < 0 else 1, rows]
            halo.append(remote(src, LK.at[3 - k], h_send, h_recv, 6 + k, corners[k]))
        halo[0].start()
        halo[1].start()
        loads[2].wait()

        @pl.loop(0, 8)
        def _(x):
            SX[0, x] = jnp.where(sub8 < 3, E[x + 3, 0:8, :], pltpu.roll(R[x + 3, 0:8, :], 3, 0))
            SX[1, x] = jnp.where(sub8 >= 5, E[x + 3, 24:32, :], pltpu.roll(R[x + 3, 24:32, :], 5, 0))

        for k in (2, 3, 6, 7, 8, 9, 4, 5):
            halo[k].start()
        announce(0)

        lane32 = iota((32, 256), 1)

        @pl.loop(3, 11)
        def _(i):
            q = E[i, 0:32, :]
            below = jnp.where(lane32 > 0, pltpu.roll(q, 1, 1), 0.0)
            above = jnp.where(lane32 < 255, pltpu.roll(q, 255, 1), 0.0)
            FZ[0, i, 0:32, :] = jnp.where(lane32 > 0, 0.5 * (below + q), 0.0)
            FZ[1, i, 0:32, :] = jnp.where(lane32 < 255, 0.5 * (above + q), 0.0)
            D[i, 0:32, :] = 3.0 * q + 0.5 * (below + above)

        @pl.loop(4, 11)
        def _(i):
            FX[i, 0:32, :] = 0.5 * (E[i - 1, 0:32, :] + E[i, 0:32, :])

        sourced = lax.fori_loop(3, 11, lambda i, acc: acc + R[i, 0:32, :], jnp.zeros((32, 256), F32))
        sourced = sourced[0:8] + sourced[8:16] + sourced[16:24] + sourced[24:32]

        heard(0)
        announce(1)
        for k in (0, 1, 2, 3, 6, 7, 8, 9):
            halo[k].wait_recv()

        def unpack(left, right, i, keep):
            right, left = right * (m_r * keep), left * (m_l * keep)
            E[i, 32:40, :] = jnp.where(sub8 < 3, right, jnp.where(sub8 >= 5, left, 0.0))
            right, left = pltpu.roll(right, 5, 0), pltpu.roll(left, 3, 0)
            R[i, 32:40, :] = jnp.where(sub8 < 2, right, jnp.where(sub8 >= 6, left, 0.0))

        @pl.loop(0, 8)
        def _(x):
            unpack(LX[0, x], LX[1, x], x + 3, 1.0)

        @pl.loop(0, 2)
        def _(x):
            unpack(LK[0, x], LK[1, x], x + 1, m_up)
            unpack(LK[2, x], LK[3, x], x + 11, m_dn)

        @pl.loop(0, 3)
        def _(x):
            E[x, 0:32, :] = E[x, 0:32, :] * m_up
            E[x + 11, 0:32, :] = E[x + 11, 0:32, :] * m_dn

        lane40, lane8 = iota((40, 256), 1), iota((8, 256), 1)

        def weigh(q, diag):
            inside = q > 0
            return jnp.where(inside, OMEGA / jnp.where(inside, diag, 1.0), 0.0)

        @pl.loop(3, 11)
        def _(i):
            q, up, dn = E[i], E[i - 1], E[i + 1]
            back, ahead_ = pltpu.roll(q, 1, 0), pltpu.roll(q, 39, 0)
            FY[0, i] = 0.5 * (back + q)
            FY[1, i] = 0.5 * (ahead_ + q)
            around = 0.5 * ((up + dn) + (back + ahead_))
            g = q[32:40]
            below = jnp.where(lane8 > 0, pltpu.roll(g, 1, 1), 0.0)
            above = jnp.where(lane8 < 255, pltpu.roll(g, 255, 1), 0.0)
            FZ[0, i, 32:40, :] = jnp.where(lane8 > 0, 0.5 * (below + g), 0.0)
            FZ[1, i, 32:40, :] = jnp.where(lane8 < 255, 0.5 * (above + g), 0.0)
            FX[i, 32:40, :] = 0.5 * (up[32:40] + g)
            diag = D[i, 0:32, :] + around[0:32]
            diag_g = 3.0 * g + 0.5 * (below + above) + around[32:40]
            w, w_g = weigh(q[0:32], diag), weigh(g, diag_g)
            D[i, 0:32, :] = diag
            W[i, 0:32, :] = w
            W[i, 32:40, :] = w_g
            PA[i, 0:32, :] = w * R[i, 0:32, :]
            PA[i, 32:40, :] = w_g * R[i, 32:40, :]

        for k in (4, 5):
            halo[k].wait_recv()

        @pl.loop(0, 2)
        def _(x):
            R[x + 1, 0:32, :] = R[x + 1, 0:32, :] * m_up
            R[x + 11, 0:32, :] = R[x + 11, 0:32, :] * m_dn

        @pl.loop(0, 4)
        def _(x):
            i = x + 1 + 8 * lax.div(x, 2)
            q = E[i]
            back, ahead_, below, above = shifted(q, 1)
            up, dn = E[i - 1], E[i + 1]
            FX[i] = 0.5 * (up + q)
            FY[0, i] = 0.5 * (back + q)
            FY[1, i] = 0.5 * (ahead_ + q)
            FZ[0, i] = jnp.where(lane40 > 0, 0.5 * (below + q), 0.0)
            FZ[1, i] = jnp.where(lane40 < 255, 0.5 * (above + q), 0.0)
            w = weigh(q, 3.0 * q + 0.5 * (((up + dn) + (back + ahead_)) + (below + above)))
            W[i] = w
            PA[i] = w * R[i]

        FX[3, 0:32, :] = 0.5 * (E[2, 0:32, :] + E[3, 0:32, :])


        def coupling(p, i, n):
            back, ahead_, below, above = rolled(p[i], 1, n)
            along = FX[i, :n] * p[i - 1, :n] + FX[i + 1, :n] * p[i + 1, :n]
            across = FY[0, i, :n] * back + FY[1, i, :n] * ahead_
            return (along + across) + (FZ[0, i, :n] * below + FZ[1, i, :n] * above)

        def spread_flat(p, i):
            v = p[i]
            along = FX[i] * p[i - 1] + FX[i + 1] * p[i + 1]
            across = FY[0, i] * pltpu.roll(v, 1, 0) + FY[1, i] * pltpu.roll(v, 39, 0)
            return (1.0 - OMEGA) * v + W[i] * ((along + across) + (FZ[0, i] + FZ[1, i]) * v)

        def spread(p, i, n):
            return (1.0 - OMEGA) * p[i, :n] + W[i, :n] * coupling(p, i, n)

        def relax(p, i, n):
            return (1.0 - OMEGA) * p[i, :n] + W[i, :n] * (R[i, :n] + coupling(p, i, n))

        @pl.loop(2, 12)
        def _(i):
            PB[i] = relax(PA, i, 40)

        left = FX[3, 0:32, :] * (PB[3, 0:32, :] - PB[2, 0:32, :])
        left = left + FX[11, 0:32, :] * (PB[10, 0:32, :] - PB[11, 0:32, :])
        left = left[0:8] + left[8:16] + left[16:24] + left[24:32]

        def faces(i, carry):
            acc, con = carry
            p, q, tile = PB[i, 0:32, :], E[i, 0:32, :], PB[i, 32:40, :]
            end = (0.5 * q) * p
            end = end[0:8] + end[8:16] + end[16:24] + end[24:32]
            acc = acc + jnp.where((lane8 == 0) | (lane8 == 255), end, 0.0)
            low = FY[0, i, 0:8, :] * (p[0:8] - pltpu.roll(tile, 1, 0))
            high = FY[1, i, 24:32, :] * (p[24:32] - pltpu.roll(tile, 7, 0))
            acc = acc + jnp.where(sub8 == 0, low, 0.0) + jnp.where(sub8 == 7, high, 0.0)
            return acc, con + E[i]

        left, con = lax.fori_loop(3, 11, faces, (left, jnp.zeros((40, 256), F32)))
        acc = sourced - left

        sub40 = iota((40, 256), 0)
        own = sub40 < 32
        down = E[9] + E[10] + E[11] + E[12]
        up = E[1] + E[2] + E[3] + E[4]
        cross = jnp.where((sub40 >= 30) & (sub40 < 34), con, 0.0)
        back = jnp.where((sub40 < 2) | (sub40 >= 38), con, 0.0)
        ends = jnp.where(own & ((lane40 < 2) | (lane40 >= 254)), con, 0.0)
        down = jnp.where(own, down, 0.0)
        outflow = 0.25 * total_of(down + jnp.where(own, up, 0.0) + cross + back + ends)
        sums = [total_of(acc), outflow, 0.25 * total_of(down), 0.25 * total_of(cross)]
        my_lane = lax.rem(z, 2) * 64 + y * 8 + me1
        here = iota((1, 128), 1) == my_lane
        for k, value in enumerate(sums):
            M1[k : k + 1, :] = jnp.where(here, value, 0.0)

        gather1 = [remote(M1, G1.at[k], s1, r1, k, group1[k]) for k in range(n1 - 1)]
        gather2 = [remote(M2, G2.at[k], s2, r2, k, group2[k]) for k in range(ny - 1)]
        gather3 = [remote(M3, G3.at[k], s3, r3, k, group3[k]) for k in range(nz - 1)]

        def launch(copies):
            middle = (len(copies) - 1) / 2
            for k in sorted(range(len(copies)), key=lambda k: abs(k - middle)):
                copies[k].start()

        launch(gather1)

        @pl.loop(0, 8)
        def _(x):
            i = x + 3
            RES[x] = R[i, :32] - D[i, :32] * PB[i, :32] + coupling(PB, i, 32)

        zero32 = jnp.zeros((32, 256), F32)
        for ref in (CC, FA, FB):
            ref[0] = zero32
            ref[5] = zero32

        @pl.loop(0, 4)
        def _(x):
            CR[x] = pair_sum(RES[2 * x] + RES[2 * x + 1])
            CC[x + 1] = 0.125 * pair_sum(E[2 * x + 3, 0:32, :] + E[2 * x + 4, 0:32, :])

        row32 = iota((32, 256), 0) % 8

        @pl.loop(1, 5)
        def _(i):
            q = CC[i]
            back, ahead_, below, above = shifted(q, 2, 8)
            up, dn = CC[i - 1], CC[i + 1]
            diag = 12.0 * q + 2.0 * (((up + dn) + (back + ahead_)) + (below + above))
            wt = OMEGA / diag
            TX[i] = 2.0 * (up + q)
            TX[i + 1] = 2.0 * (dn + q)
            TY[0, i] = jnp.where(row32 >= 2, 2.0 * (back + q), 0.0)
            TY[1, i] = jnp.where(row32 < 6, 2.0 * (ahead_ + q), 0.0)
            TZ[0, i] = jnp.where(lane32 >= 2, 2.0 * (below + q), 0.0)
            TZ[1, i] = jnp.where(lane32 < 254, 2.0 * (above + q), 0.0)
            WT[i] = wt
            FA[i] = wt * CR[i - 1]

        def tile_relax(f, i):
            v = f[i]
            back, ahead_, below, above = rolled(v, 2, 32)
            along = TX[i] * f[i - 1] + TX[i + 1] * f[i + 1]
            across = TY[0, i] * back + TY[1, i] * ahead_
            around = (along + across) + (TZ[0, i] * below + TZ[1, i] * above)
            return (1.0 - OMEGA) * v + WT[i] * (CR[i - 1] + around)

        f, g = FA, FB
        for sweep in range(BLOCK_SWEEPS - 1):

            @pl.loop(1, 5)
            def _(i, f=f, g=g):
                g[i] = tile_relax(f, i)

            f, g = g, f

        tile_of_row = iota((32, 256), 0) // 8
        cloud = jnp.zeros((32, 256), F32)
        for t in range(4):
            cloud = jnp.where(tile_of_row == t, flag(route[0, t] >= 0), cloud)

        @pl.loop(0, 4)
        def _(x):
            fix = f[x + 1] * cloud
            Q[2 * x + 3, 0:32, :] = PB[2 * x + 3, 0:32, :] + fix
            Q[2 * x + 4, 0:32, :] = PB[2 * x + 4, 0:32, :] + fix

        heard(1)
        announce(2)
        for copy in gather1:
            copy.wait_recv()
        row = M1[...]
        for k in range(n1 - 1):
            row = row + G1[k]
        M2[...] = row
        launch(gather2)

        src_rows = {-1: slice(3, 5), 1: slice(9, 11)}
        dst_rows = {-1: slice(11, 13), 1: slice(1, 3)}
        src_cols = {-1: slice(0, 8), 1: slice(24, 32)}
        mid, band = slice(3, 11), slice(0, 32)
        fix_halo = []
        for k, sx in enumerate((-1, 1)):
            src, dst = Q.at[src_rows[sx], band, :], Q.at[dst_rows[sx], band, :]
            fix_halo.append(remote(src, dst, q_send, q_recv, k, near[k]))
        for k, sy in enumerate((-1, 1)):
            src = Q.at[mid, src_cols[sy], :]
            fix_halo.append(remote(src, QX.at[1 - k], q_send, q_recv, 2 + k, near[2 + k]))
        for k, (sx, sy) in enumerate(CORNERS):
            src = Q.at[3 if sx < 0 else 10, src_cols[sy], :]
            fix_halo.append(remote(src, QK.at[3 - k], q_send, q_recv, 4 + k, corners[k]))
        for copy in fix_halo:
            copy.start()

        zero32 = jnp.zeros((32, 256), F32)
        zero40 = jnp.zeros((40, 256), F32)
        side = jnp.where(sub8 < 4, m_r, m_l) + zero8

        def ones(i, band_value, tile_value):
            U[i, 0:32, :] = zero32 + band_value
            U[i, 32:40, :] = side * tile_value

        def set_ones(inner, inner_side, outer, outer_side):
            for i, keep in ((1, m_up), (2, m_up), (11, m_dn), (12, m_dn)):
                ones(i, outer * keep, outer_side * keep)

            @pl.loop(3, 11)
            def _(i):
                ones(i, inner, inner_side)

        set_ones(1.0, 1.0, 1.0, 1.0)

        @pl.loop(2, 12)
        def _(i):
            V[i] = spread_flat(U, i)

        @pl.loop(3, 11)
        def _(i):
            GA[i - 3] = spread(V, i, 32)

        def cut(ref, *at):
            return jnp.concatenate([ref[(*at, slice(24, 40))], ref[(*at, slice(0, 8))]], axis=0)

        beside_one = jnp.concatenate([zero8, side, zero8], axis=0)
        for i in (2, 11):
            S[i] = jnp.zeros((24, 256), F32)

        @pl.loop(3, 11)
        def _(i):
            along = cut(FX, i) * flag(i > 3) + cut(FX, i + 1) * flag(i < 10)
            column = cut(FZ, 0, i) + cut(FZ, 1, i)
            back, ahead_ = pltpu.roll(beside_one, 1, 0), pltpu.roll(beside_one, 23, 0)
            across = cut(FY, 0, i) * back + cut(FY, 1, i) * ahead_
            total = (along + column) * beside_one + across
            S[i] = (1.0 - OMEGA) * beside_one + cut(W, i) * total

        @pl.loop(3, 11)
        def _(i):
            v = S[i]
            back, ahead_, below, above = rolled(v, 1, 24)
            along = cut(FX, i) * S[i - 1] + cut(FX, i + 1) * S[i + 1]
            across = cut(FY, 0, i) * back + cut(FY, 1, i) * ahead_
            column = cut(FZ, 0, i) * below + cut(FZ, 1, i) * above
            v = (1.0 - OMEGA) * v + cut(W, i) * ((along + across) + column)
            GS[i - 3, 0:8, :] = v[16:24]
            GS[i - 3, 8:16, :] = v[0:8]

        for i in (4, 5, 8, 9):
            V[i] = zero40
        for target, outer, rows in ((GD, 1.0, (3, 4, 9, 10)), (GC, 0.0, (3, 10))):
            set_ones(0.0, 0.0, outer, 1.0 - outer)
            for i in (2, 3, 10, 11):
                V[i] = spread_flat(U, i)
            for k, i in enumerate(rows):
                target[k] = spread(V, i, 32)

        for copy in gather2:
            copy.wait_recv()
        row = M2[...]
        for k in range(ny - 1):
            row = row + G2[k]
        M3[...] = row
        heard(2)
        launch(gather3)
        for copy in fix_halo:
            copy.wait_recv()

        for lo, hi, keep in ((1, 3, m_up), (3, 11, 1.0), (11, 13, m_dn)):

            @pl.loop(lo, hi)
            def _(i, keep=keep):
                PA[i, 0:32, :] = Q[i, 0:32, :] * keep

        def beside_tile(left, right, keep):
            return jnp.where(sub8 < 4, right * m_r, left * m_l) * keep

        @pl.loop(0, 8)
        def _(x):
            PA[x + 3, 32:40, :] = beside_tile(QX[0, x], QX[1, x], 1.0)

        PA[1, 32:40, :] = zero8
        PA[2, 32:40, :] = beside_tile(QK[0], QK[1], m_up)
        PA[11, 32:40, :] = beside_tile(QK[2], QK[3], m_dn)
        PA[12, 32:40, :] = zero8

        @pl.loop(2, 12)
        def _(i):
            PB[i] = relax(PA, i, 40)

        @pl.loop(3, 11)
        def _(i):
            out[i - 3] = relax(PB, i, 32)

        sub, lane = iota((8, 128), 0), iota((8, 128), 1)
        tz = 2 * sub + lane // 64
        ty = (lane % 64) // 8
        tc = (lane % 8) // 2
        odd = lane % 2 == 1

        for copy in halo + gather1 + gather2 + fix_halo + gather3:
            copy.wait_send()
        table = [jnp.where(sub == lax.div(z, 2), M3[k : k + 1, :], 0.0) for k in range(4)]
        for j in sorted(range(nz - 1), key=lambda j: -abs(j - (nz - 2) / 2)):
            from_z = lax.rem(z + nz - 1 - j, nz)
            at = sub == lax.div(from_z, 2)
            gather3[j].wait_recv()
            for k in range(4):
                table[k] = table[k] + jnp.where(at, G3[j, k : k + 1, :], 0.0)
        totals, outs, link_dn, link_cr = table

        def ahead(value, by):
            return pltpu.roll(value, (-by) % 128, 1)

        def shift_rows(value, by):
            return pltpu.roll(value, by % 8, 0)

        def next_parts(value):
            v63 = ahead(value, 63)
            return ahead(value, 1), v63, shift_rows(v63, -1), shift_rows(ahead(value, 71), half - 1)

        def prev_parts(value):
            v63 = ahead(value, -63)
            return (
                ahead(value, -1), v63, shift_rows(v63, 1), shift_rows(ahead(value, -71), 1 - half)
            )

        last = (ty == ny - 1) & (tz == nz - 1)
        first = (ty == 0) & (tz == 0)
        next_at = (
            ~odd,
            odd & (tz % 2 == 0),
            odd & (tz % 2 == 1) & (tz < nz - 1),
            odd & (tz == nz - 1) & ~last,
        )
        prev_at = (
            odd,
            ~odd & (tz % 2 == 1),
            ~odd & (tz % 2 == 0) & (tz > 0),
            ~odd & (tz == 0) & ~first,
        )
        link_up = jnp.zeros((8, 128), F32)
        held = (tz < nz) & (ty < ny) & (tc < n_cross)
        for at, part in zip(prev_at, prev_parts(link_dn)):
            link_up = jnp.where(at & held, part, link_up)
        link_bk = jnp.where((tc > 0) & held, ahead(link_cr, -2), 0.0)
        link_cr = jnp.where(tc < n_cross - 1, link_cr, 0.0)
        next_w = [jnp.where(at, link_dn, 0.0) for at in next_at]
        prev_w = [jnp.where(at, link_up, 0.0) for at in prev_at]

        def operate(value):
            image = outs * value - link_cr * ahead(value, 2) - link_bk * ahead(value, -2)
            for weight, part in zip(next_w, next_parts(value)):
                image = image - weight * part
            for weight, part in zip(prev_w, prev_parts(value)):
                image = image - weight * part
            return image

        def iterate(step, carry):
            answer, resid, search, image, over_norm, over_alpha = carry
            shown = operate(resid)
            norm = total_of(resid * resid)
            weight = total_of(resid * shown)
            beta = norm * over_norm
            alpha = norm / (weight - beta * (norm * over_alpha))
            search = resid + beta * search
            image = shown + beta * image
            answer = answer + alpha * search
            resid = resid - alpha * image
            return answer, resid, search, image, 1.0 / norm, 1.0 / alpha

        none, nil = jnp.zeros((8, 128), F32), jnp.zeros((1, 1), F32)
        start = (none, totals, none, none, nil, nil)
        answer = lax.fori_loop(0, COARSE_ITERS, iterate, start)[0]

        def brick(dd, cc):
            core_b, chip_b = lax.rem(dd, 2), lax.div(dd, 2)
            z_b, y_b = lax.rem(chip_b, nz), lax.div(chip_b, nz)
            at_lane = lax.rem(z_b, 2) * 64 + y_b * 8 + cc * 2 + core_b
            return total_of(jnp.where((sub == lax.div(z_b, 2)) & (lane == at_lane), answer, 0.0))

        mine = brick(d, c)
        near_by = [brick(dd, cc) - mine for dd, cc in near]
        at_corner = [brick(dd, cc) - mine for dd, cc in corners]
        first_half = iota((32, 256), 0) < 16

        @pl.loop(0, 8)
        def _(x):
            out[x, 8:24, :] = out[x, 8:24, :] + mine * GA[x, 8:24, :]
            low, high = out[x, 0:8, :], out[x, 24:32, :]
            out[x, 0:8, :] = low + (mine * GA[x, 0:8, :] + near_by[2] * GS[x, 0:8, :])
            out[x, 24:32, :] = high + (mine * GA[x, 24:32, :] + near_by[3] * GS[x, 8:16, :])

        for k, x in enumerate((0, 1, 6, 7)):
            out[x] = out[x] + near_by[k // 2] * GD[k]
        for k, x in enumerate((0, 7)):
            out[x] = out[x] + jnp.where(first_half, at_corner[2 * k], at_corner[2 * k + 1]) * GC[k]


    return kernel


def solution(mesh):
    n_down, n_cross = mesh.shape["down"], mesh.shape["cross"]
    nz = CHIPS_Z
    ny = n_down // (2 * nz)
    n1 = 2 * n_cross
    big = pltpu.VMEM((14, 40, 256), F32)
    two = pltpu.VMEM((2, 14, 40, 256), F32)
    coarse = pltpu.VMEM((6, 32, 256), F32)
    coarse2 = pltpu.VMEM((2, 6, 32, 256), F32)
    dma = pltpu.SemaphoreType.DMA
    msg = pltpu.VMEM((4, 128), F32)

    def body(right_side, kappa, band_mask, tile_route):
        return pl.pallas_call(
            make_kernel(n_down, n_cross, nz),
            out_shape=pltpu.VMEM(right_side.shape, F32),
            in_specs=[pl.BlockSpec(memory_space=pl.ANY)] * 3
            + [pl.BlockSpec(memory_space=pltpu.SMEM)],
            out_specs=pl.BlockSpec(memory_space=pltpu.VMEM),
            scratch_shapes=[
                big, big, pltpu.VMEM((8, 32, 256), jnp.int32), big, big, big, big, big,
                big, two, two,
                pltpu.VMEM((8, 32, 256), F32),
                pltpu.VMEM((4, 32, 256), F32), coarse, coarse, coarse, coarse2, coarse2,
                coarse, coarse,
                pltpu.VMEM((2, 8, 8, 256), F32), pltpu.VMEM((2, 8, 8, 256), F32),
                pltpu.VMEM((4, 2, 8, 256), F32),
                pltpu.VMEM((2, 8, 8, 256), F32), pltpu.VMEM((4, 8, 256), F32),
                big, big, pltpu.VMEM((14, 24, 256), F32),
                pltpu.VMEM((8, 32, 256), F32), pltpu.VMEM((8, 16, 256), F32),
                pltpu.VMEM((4, 32, 256), F32), pltpu.VMEM((2, 32, 256), F32),
                msg, pltpu.VMEM((n1 - 1, 4, 128), F32),
                msg, pltpu.VMEM((ny - 1, 4, 128), F32),
                msg, pltpu.VMEM((nz - 1, 4, 128), F32),
                dma((3,)), dma((10,)), dma((10,)), dma((8,)), dma((8,)),
                dma((n1 - 1,)), dma((n1 - 1,)), dma((ny - 1,)), dma((ny - 1,)),
                dma((nz - 1,)), dma((nz - 1,)), pltpu.SemaphoreType.REGULAR((3,)),
            ],
            compiler_params=pltpu.CompilerParams(collective_id=0, has_side_effects=True),
            name="cycle",
        )(right_side, kappa, band_mask, tile_route)

    return jax.shard_map(
        body,
        mesh=mesh,
        in_specs=(
            P("down", "cross", None),
            P("down", "cross", None),
            P("down", "cross", None),
            P("down", "cross"),
        ),
        out_specs=P("down", "cross", None),
        check_vma=False,
    )
```

```python
import jax
import jax.numpy as jnp
from jax import lax
from jax.experimental import pallas as pl
from jax.experimental.pallas import tpu as pltpu
from jax.sharding import PartitionSpec as P

OMEGA = 0.8
BLOCK_SWEEPS = 4
COARSE_ITERS = 12
CHIPS_Z = 12

MESH = pl.DeviceIdType.MESH
CORNERS = ((-1, -1), (-1, 1), (1, -1), (1, 1))
F32 = jnp.float32


def iota(shape, dim):
    return lax.broadcasted_iota(jnp.int32, shape, dim)


def flag(cond):
    return jnp.where(cond, 1.0, 0.0).astype(F32)


def total_of(value):
    return jnp.sum(jnp.sum(value, axis=0, keepdims=True), axis=1, keepdims=True)


def shifted(value, by, tile=0):
    rows, lanes = value.shape
    row, lane = iota(value.shape, 0) % max(tile, 1), iota(value.shape, 1)
    back, ahead = pltpu.roll(value, by, 0), pltpu.roll(value, rows - by, 0)
    if tile:
        back = jnp.where(row >= by, back, 0.0)
        ahead = jnp.where(row < tile - by, ahead, 0.0)
    below = jnp.where(lane >= by, pltpu.roll(value, by, 1), 0.0)
    above = jnp.where(lane < lanes - by, pltpu.roll(value, lanes - by, 1), 0.0)
    return back, ahead, below, above


def rolled(value, by, rows_out):
    rows, lanes = value.shape
    return (
        pltpu.roll(value, by, 0)[:rows_out],
        pltpu.roll(value, rows - by, 0)[:rows_out],
        pltpu.roll(value[:rows_out], by, 1),
        pltpu.roll(value[:rows_out], lanes - by, 1),
    )


def pair_sum(value):
    rows, lanes = value.shape
    row, lane = iota(value.shape, 0), iota(value.shape, 1)
    value = value + jnp.where(row % 2 == 0, pltpu.roll(value, rows - 1, 0), pltpu.roll(value, 1, 0))
    return value + jnp.where(
        lane % 2 == 0, pltpu.roll(value, lanes - 1, 1), pltpu.roll(value, 1, 1)
    )


def make_kernel(n_down, n_cross, nz):
    ny = n_down // (2 * nz)
    half = nz // 2

    def kernel(
        rhs_hbm, kappa_hbm, mask_hbm, route, out,
        E, R, MK, D, W, PA, PB, Q, FX, FY, FZ, RES, CR, CC, WT, TX, TY, TZ, FA, FB,
        SX, LX, LK, QX, QK, U, V, S, GA, GS, GD, GC, M1, G1, M2, G2, M3, G3,
        load_sem, h_send, h_recv, q_send, q_recv,
        s1, r1, s2, r2, s3, r3, chain,
    ):
        d = lax.axis_index("down")
        c = lax.axis_index("cross")
        core = lax.rem(d, 2)
        chip = lax.div(d, 2)
        z = lax.rem(chip, nz)
        y = lax.div(chip, nz)

        loads = [
            pltpu.make_async_copy(kappa_hbm, E.at[3:11, 0:32, :], load_sem.at[0]),
            pltpu.make_async_copy(mask_hbm, MK, load_sem.at[1]),
            pltpu.make_async_copy(rhs_hbm, R.at[3:11, 0:32, :], load_sem.at[2]),
        ]
        for load in loads:
            load.start()

        d_next, d_prev = lax.rem(d + 1, n_down), lax.rem(d + n_down - 1, n_down)
        c_next, c_prev = lax.rem(c + 1, n_cross), lax.rem(c + n_cross - 1, n_cross)
        near = [(d_prev, c), (d_next, c), (d, c_prev), (d, c_next)]
        corners = [
            (d_prev if sx < 0 else d_next, c_prev if sy < 0 else c_next) for sx, sy in CORNERS
        ]
        n1 = 2 * n_cross
        me1 = c * 2 + core
        group1 = []
        for k in range(1, n1):
            g = lax.rem(me1 + k, n1)
            group1.append((chip * 2 + lax.rem(g, 2), lax.div(g, 2)))
        group2 = [((lax.rem(y + k, ny) * nz + z) * 2 + core, c) for k in range(1, ny)]
        group3 = [((y * nz + lax.rem(z + k, nz)) * 2 + core, c) for k in range(1, nz)]

        barrier = pltpu.get_barrier_semaphore()
        def at_z(by):
            return ((y * nz + lax.rem(z + nz + by, nz)) * 2 + core, c)

        def at_y(by):
            return ((lax.rem(y + ny + by, ny) * nz + z) * 2 + core, c)

        beside = [at_z(1), at_z(-1), at_y(1), at_y(-1)]
        rounds = [beside, [at_z(2), at_z(-2), at_y(2), at_y(-2)], [at_z(2), at_z(-2)]]
        peers = near + corners + group1 + beside
        for peer in peers:
            pl.semaphore_signal(barrier, inc=1, device_id=peer, device_id_type=MESH)

        m_up, m_dn = flag(d > 0), flag(d < n_down - 1)
        m_l, m_r = flag(c > 0), flag(c < n_cross - 1)

        zero8 = jnp.zeros((8, 256), F32)
        for i in (0, 13):
            E[i, 32:40, :] = zero8
        loads[0].wait()
        loads[1].wait()

        @pl.loop(0, 8)
        def _(x):
            kap = E[x + 3, 0:32, :]
            E[x + 3, 0:32, :] = jnp.where(MK[x] > 0, kap * 0.25, kap)

        sub8 = iota((8, 256), 0)

        pl.semaphore_wait(barrier, len(peers))

        def announce(k):
            for peer in rounds[k]:
                pl.semaphore_signal(chain.at[k], inc=1, device_id=peer, device_id_type=MESH)

        def heard(k):
            pl.semaphore_wait(chain.at[k], len(rounds[k]))

        def remote(src, dst, send, recv, k, peer):
            return pltpu.make_async_remote_copy(
                src_ref=src, dst_ref=dst, send_sem=send.at[k], recv_sem=recv.at[k],
                device_id=peer, device_id_type=MESH,
            )

        halo = [
            remote(E.at[3:6, 0:32, :], E.at[11:14, 0:32, :], h_send, h_recv, 0, near[0]),
            remote(E.at[8:11, 0:32, :], E.at[0:3, 0:32, :], h_send, h_recv, 1, near[1]),
            remote(SX.at[0], LX.at[1], h_send, h_recv, 2, near[2]),
            remote(SX.at[1], LX.at[0], h_send, h_recv, 3, near[3]),
            remote(R.at[3:5, 0:32, :], R.at[11:13, 0:32, :], h_send, h_recv, 4, near[0]),
            remote(R.at[9:11, 0:32, :], R.at[1:3, 0:32, :], h_send, h_recv, 5, near[1]),
        ]
        for k, (sx, sy) in enumerate(CORNERS):
            rows = slice(0, 2) if sx < 0 else slice(6, 8)
            src = SX.at[0 if sy < 0 else 1, rows]
            halo.append(remote(src, LK.at[3 - k], h_send, h_recv, 6 + k, corners[k]))
        halo[0].start()
        halo[1].start()
        loads[2].wait()

        @pl.loop(0, 8)
        def _(x):
            SX[0, x] = jnp.where(sub8 < 3, E[x + 3, 0:8, :], pltpu.roll(R[x + 3, 0:8, :], 3, 0))
            SX[1, x] = jnp.where(sub8 >= 5, E[x + 3, 24:32, :], pltpu.roll(R[x + 3, 24:32, :], 5, 0))

        for k in (2, 3, 6, 7, 8, 9, 4, 5):
            halo[k].start()
        announce(0)

        lane32 = iota((32, 256), 1)

        @pl.loop(3, 11)
        def _(i):
            q = E[i, 0:32, :]
            below = jnp.where(lane32 > 0, pltpu.roll(q, 1, 1), 0.0)
            above = jnp.where(lane32 < 255, pltpu.roll(q, 255, 1), 0.0)
            FZ[0, i, 0:32, :] = jnp.where(lane32 > 0, 0.5 * (below + q), 0.0)
            FZ[1, i, 0:32, :] = jnp.where(lane32 < 255, 0.5 * (above + q), 0.0)
            D[i, 0:32, :] = 3.0 * q + 0.5 * (below + above)

        @pl.loop(4, 11)
        def _(i):
            FX[i, 0:32, :] = 0.5 * (E[i - 1, 0:32, :] + E[i, 0:32, :])

        sourced = lax.fori_loop(3, 11, lambda i, acc: acc + R[i, 0:32, :], jnp.zeros((32, 256), F32))
        sourced = sourced[0:8] + sourced[8:16] + sourced[16:24] + sourced[24:32]

        heard(0)
        announce(1)
        for k in (0, 1, 2, 3, 6, 7, 8, 9):
            halo[k].wait_recv()

        def unpack(left, right, i, keep):
            right, left = right * (m_r * keep), left * (m_l * keep)
            E[i, 32:40, :] = jnp.where(sub8 < 3, right, jnp.where(sub8 >= 5, left, 0.0))
            right, left = pltpu.roll(right, 5, 0), pltpu.roll(left, 3, 0)
            R[i, 32:40, :] = jnp.where(sub8 < 2, right, jnp.where(sub8 >= 6, left, 0.0))

        @pl.loop(0, 8)
        def _(x):
            unpack(LX[0, x], LX[1, x], x + 3, 1.0)

        @pl.loop(0, 2)
        def _(x):
            unpack(LK[0, x], LK[1, x], x + 1, m_up)
            unpack(LK[2, x], LK[3, x], x + 11, m_dn)

        @pl.loop(0, 3)
        def _(x):
            E[x, 0:32, :] = E[x, 0:32, :] * m_up
            E[x + 11, 0:32, :] = E[x + 11, 0:32, :] * m_dn

        lane40, lane8 = iota((40, 256), 1), iota((8, 256), 1)

        def weigh(q, diag):
            inside = q > 0
            return jnp.where(inside, OMEGA / jnp.where(inside, diag, 1.0), 0.0)

        @pl.loop(3, 11)
        def _(i):
            q, up, dn = E[i], E[i - 1], E[i + 1]
            back, ahead_ = pltpu.roll(q, 1, 0), pltpu.roll(q, 39, 0)
            FY[0, i] = 0.5 * (back + q)
            FY[1, i] = 0.5 * (ahead_ + q)
            around = 0.5 * ((up + dn) + (back + ahead_))
            g = q[32:40]
            below = jnp.where(lane8 > 0, pltpu.roll(g, 1, 1), 0.0)
            above = jnp.where(lane8 < 255, pltpu.roll(g, 255, 1), 0.0)
            FZ[0, i, 32:40, :] = jnp.where(lane8 > 0, 0.5 * (below + g), 0.0)
            FZ[1, i, 32:40, :] = jnp.where(lane8 < 255, 0.5 * (above + g), 0.0)
            FX[i, 32:40, :] = 0.5 * (up[32:40] + g)
            diag = D[i, 0:32, :] + around[0:32]
            diag_g = 3.0 * g + 0.5 * (below + above) + around[32:40]
            w, w_g = weigh(q[0:32], diag), weigh(g, diag_g)
            D[i, 0:32, :] = diag
            W[i, 0:32, :] = w
            W[i, 32:40, :] = w_g
            PA[i, 0:32, :] = w * R[i, 0:32, :]
            PA[i, 32:40, :] = w_g * R[i, 32:40, :]

        for k in (4, 5):
            halo[k].wait_recv()

        @pl.loop(0, 2)
        def _(x):
            R[x + 1, 0:32, :] = R[x + 1, 0:32, :] * m_up
            R[x + 11, 0:32, :] = R[x + 11, 0:32, :] * m_dn

        @pl.loop(0, 4)
        def _(x):
            i = x + 1 + 8 * lax.div(x, 2)
            q = E[i]
            back, ahead_, below, above = shifted(q, 1)
            up, dn = E[i - 1], E[i + 1]
            FX[i] = 0.5 * (up + q)
            FY[0, i] = 0.5 * (back + q)
            FY[1, i] = 0.5 * (ahead_ + q)
            FZ[0, i] = jnp.where(lane40 > 0, 0.5 * (below + q), 0.0)
            FZ[1, i] = jnp.where(lane40 < 255, 0.5 * (above + q), 0.0)
            w = weigh(q, 3.0 * q + 0.5 * (((up + dn) + (back + ahead_)) + (below + above)))
            W[i] = w
            PA[i] = w * R[i]

        FX[3, 0:32, :] = 0.5 * (E[2, 0:32, :] + E[3, 0:32, :])


        def coupling(p, i, n):
            back, ahead_, below, above = rolled(p[i], 1, n)
            along = FX[i, :n] * p[i - 1, :n] + FX[i + 1, :n] * p[i + 1, :n]
            across = FY[0, i, :n] * back + FY[1, i, :n] * ahead_
            return (along + across) + (FZ[0, i, :n] * below + FZ[1, i, :n] * above)

        def spread_flat(p, i):
            v = p[i]
            along = FX[i] * p[i - 1] + FX[i + 1] * p[i + 1]
            across = FY[0, i] * pltpu.roll(v, 1, 0) + FY[1, i] * pltpu.roll(v, 39, 0)
            return (1.0 - OMEGA) * v + W[i] * ((along + across) + (FZ[0, i] + FZ[1, i]) * v)

        def spread(p, i, n):
            return (1.0 - OMEGA) * p[i, :n] + W[i, :n] * coupling(p, i, n)

        def relax(p, i, n):
            return (1.0 - OMEGA) * p[i, :n] + W[i, :n] * (R[i, :n] + coupling(p, i, n))

        @pl.loop(2, 12)
        def _(i):
            PB[i] = relax(PA, i, 40)

        left = FX[3, 0:32, :] * (PB[3, 0:32, :] - PB[2, 0:32, :])
        left = left + FX[11, 0:32, :] * (PB[10, 0:32, :] - PB[11, 0:32, :])
        left = left[0:8] + left[8:16] + left[16:24] + left[24:32]

        def faces(i, carry):
            acc, con = carry
            p, q, tile = PB[i, 0:32, :], E[i, 0:32, :], PB[i, 32:40, :]
            end = (0.5 * q) * p
            end = end[0:8] + end[8:16] + end[16:24] + end[24:32]
            acc = acc + jnp.where((lane8 == 0) | (lane8 == 255), end, 0.0)
            low = FY[0, i, 0:8, :] * (p[0:8] - pltpu.roll(tile, 1, 0))
            high = FY[1, i, 24:32, :] * (p[24:32] - pltpu.roll(tile, 7, 0))
            acc = acc + jnp.where(sub8 == 0, low, 0.0) + jnp.where(sub8 == 7, high, 0.0)
            return acc, con + E[i]

        left, con = lax.fori_loop(3, 11, faces, (left, jnp.zeros((40, 256), F32)))
        acc = sourced - left

        sub40 = iota((40, 256), 0)
        own = sub40 < 32
        down = E[9] + E[10] + E[11] + E[12]
        up = E[1] + E[2] + E[3] + E[4]
        cross = jnp.where((sub40 >= 30) & (sub40 < 34), con, 0.0)
        back = jnp.where((sub40 < 2) | (sub40 >= 38), con, 0.0)
        ends = jnp.where(own & ((lane40 < 2) | (lane40 >= 254)), con, 0.0)
        down = jnp.where(own, down, 0.0)
        outflow = 0.25 * total_of(down + jnp.where(own, up, 0.0) + cross + back + ends)
        sums = [total_of(acc), outflow, 0.25 * total_of(down), 0.25 * total_of(cross)]
        my_lane = lax.rem(z, 2) * 64 + y * 8 + me1
        here = iota((1, 128), 1) == my_lane
        for k, value in enumerate(sums):
            M1[k : k + 1, :] = jnp.where(here, value, 0.0)

        gather1 = [remote(M1, G1.at[k], s1, r1, k, group1[k]) for k in range(n1 - 1)]
        gather2 = [remote(M2, G2.at[k], s2, r2, k, group2[k]) for k in range(ny - 1)]
        gather3 = [remote(M3, G3.at[k], s3, r3, k, group3[k]) for k in range(nz - 1)]

        def launch(copies):
            middle = (len(copies) - 1) / 2
            for k in sorted(range(len(copies)), key=lambda k: abs(k - middle)):
                copies[k].start()

        launch(gather1)

        @pl.loop(0, 8)
        def _(x):
            i = x + 3
            RES[x] = R[i, :32] - D[i, :32] * PB[i, :32] + coupling(PB, i, 32)

        zero32 = jnp.zeros((32, 256), F32)
        for ref in (CC, FA, FB):
            ref[0] = zero32
            ref[5] = zero32

        @pl.loop(0, 4)
        def _(x):
            CR[x] = pair_sum(RES[2 * x] + RES[2 * x + 1])
            CC[x + 1] = 0.125 * pair_sum(E[2 * x + 3, 0:32, :] + E[2 * x + 4, 0:32, :])

        row32 = iota((32, 256), 0) % 8

        @pl.loop(1, 5)
        def _(i):
            q = CC[i]
            back, ahead_, below, above = shifted(q, 2, 8)
            up, dn = CC[i - 1], CC[i + 1]
            diag = 12.0 * q + 2.0 * (((up + dn) + (back + ahead_)) + (below + above))
            wt = OMEGA / diag
            TX[i] = 2.0 * (up + q)
            TX[i + 1] = 2.0 * (dn + q)
            TY[0, i] = jnp.where(row32 >= 2, 2.0 * (back + q), 0.0)
            TY[1, i] = jnp.where(row32 < 6, 2.0 * (ahead_ + q), 0.0)
            TZ[0, i] = jnp.where(lane32 >= 2, 2.0 * (below + q), 0.0)
            TZ[1, i] = jnp.where(lane32 < 254, 2.0 * (above + q), 0.0)
            WT[i] = wt
            FA[i] = wt * CR[i - 1]

        def tile_relax(f, i):
            v = f[i]
            back, ahead_, below, above = rolled(v, 2, 32)
            along = TX[i] * f[i - 1] + TX[i + 1] * f[i + 1]
            across = TY[0, i] * back + TY[1, i] * ahead_
            around = (along + across) + (TZ[0, i] * below + TZ[1, i] * above)
            return (1.0 - OMEGA) * v + WT[i] * (CR[i - 1] + around)

        f, g = FA, FB
        for sweep in range(BLOCK_SWEEPS - 1):

            @pl.loop(1, 5)
            def _(i, f=f, g=g):
                g[i] = tile_relax(f, i)

            f, g = g, f

        tile_of_row = iota((32, 256), 0) // 8
        cloud = jnp.zeros((32, 256), F32)
        for t in range(4):
            cloud = jnp.where(tile_of_row == t, flag(route[0, t] >= 0), cloud)

        @pl.loop(0, 4)
        def _(x):
            fix = f[x + 1] * cloud
            Q[2 * x + 3, 0:32, :] = PB[2 * x + 3, 0:32, :] + fix
            Q[2 * x + 4, 0:32, :] = PB[2 * x + 4, 0:32, :] + fix

        heard(1)
        announce(2)
        for copy in gather1:
            copy.wait_recv()
        row = M1[...]
        for k in range(n1 - 1):
            row = row + G1[k]
        M2[...] = row
        launch(gather2)

        src_rows = {-1: slice(3, 5), 1: slice(9, 11)}
        dst_rows = {-1: slice(11, 13), 1: slice(1, 3)}
        src_cols = {-1: slice(0, 8), 1: slice(24, 32)}
        mid, band = slice(3, 11), slice(0, 32)
        fix_halo = []
        for k, sx in enumerate((-1, 1)):
            src, dst = Q.at[src_rows[sx], band, :], Q.at[dst_rows[sx], band, :]
            fix_halo.append(remote(src, dst, q_send, q_recv, k, near[k]))
        for k, sy in enumerate((-1, 1)):
            src = Q.at[mid, src_cols[sy], :]
            fix_halo.append(remote(src, QX.at[1 - k], q_send, q_recv, 2 + k, near[2 + k]))
        for k, (sx, sy) in enumerate(CORNERS):
            src = Q.at[3 if sx < 0 else 10, src_cols[sy], :]
            fix_halo.append(remote(src, QK.at[3 - k], q_send, q_recv, 4 + k, corners[k]))
        for copy in fix_halo:
            copy.start()

        zero32 = jnp.zeros((32, 256), F32)
        zero40 = jnp.zeros((40, 256), F32)
        side = jnp.where(sub8 < 4, m_r, m_l) + zero8

        def ones(i, band_value, tile_value):
            U[i, 0:32, :] = zero32 + band_value
            U[i, 32:40, :] = side * tile_value

        def set_ones(inner, inner_side, outer, outer_side):
            for i, keep in ((1, m_up), (2, m_up), (11, m_dn), (12, m_dn)):
                ones(i, outer * keep, outer_side * keep)

            @pl.loop(3, 11)
            def _(i):
                ones(i, inner, inner_side)

        set_ones(1.0, 1.0, 1.0, 1.0)

        @pl.loop(2, 12)
        def _(i):
            V[i] = spread_flat(U, i)

        @pl.loop(3, 11)
        def _(i):
            GA[i - 3] = spread(V, i, 32)

        def cut(ref, *at):
            return jnp.concatenate([ref[(*at, slice(24, 40))], ref[(*at, slice(0, 8))]], axis=0)

        beside_one = jnp.concatenate([zero8, side, zero8], axis=0)
        for i in (2, 11):
            S[i] = jnp.zeros((24, 256), F32)

        @pl.loop(3, 11)
        def _(i):
            along = cut(FX, i) * flag(i > 3) + cut(FX, i + 1) * flag(i < 10)
            column = cut(FZ, 0, i) + cut(FZ, 1, i)
            back, ahead_ = pltpu.roll(beside_one, 1, 0), pltpu.roll(beside_one, 23, 0)
            across = cut(FY, 0, i) * back + cut(FY, 1, i) * ahead_
            total = (along + column) * beside_one + across
            S[i] = (1.0 - OMEGA) * beside_one + cut(W, i) * total

        @pl.loop(3, 11)
        def _(i):
            v = S[i]
            back, ahead_, below, above = rolled(v, 1, 24)
            along = cut(FX, i) * S[i - 1] + cut(FX, i + 1) * S[i + 1]
            across = cut(FY, 0, i) * back + cut(FY, 1, i) * ahead_
            column = cut(FZ, 0, i) * below + cut(FZ, 1, i) * above
            v = (1.0 - OMEGA) * v + cut(W, i) * ((along + across) + column)
            GS[i - 3, 0:8, :] = v[16:24]
            GS[i - 3, 8:16, :] = v[0:8]

        for copy in gather2:
            copy.wait_recv()
        row = M2[...]
        for k in range(ny - 1):
            row = row + G2[k]
        M3[...] = row
        heard(2)
        launch(gather3)
        for i in (4, 5, 8, 9):
            V[i] = zero40
        for target, outer, rows in ((GD, 1.0, (3, 4, 9, 10)), (GC, 0.0, (3, 10))):
            set_ones(0.0, 0.0, outer, 1.0 - outer)
            for i in (2, 3, 10, 11):
                V[i] = spread_flat(U, i)
            for k, i in enumerate(rows):
                target[k] = spread(V, i, 32)
        for copy in fix_halo:
            copy.wait_recv()

        for lo, hi, keep in ((1, 3, m_up), (3, 11, 1.0), (11, 13, m_dn)):

            @pl.loop(lo, hi)
            def _(i, keep=keep):
                PA[i, 0:32, :] = Q[i, 0:32, :] * keep

        def beside_tile(left, right, keep):
            return jnp.where(sub8 < 4, right * m_r, left * m_l) * keep

        @pl.loop(0, 8)
        def _(x):
            PA[x + 3, 32:40, :] = beside_tile(QX[0, x], QX[1, x], 1.0)

        PA[1, 32:40, :] = zero8
        PA[2, 32:40, :] = beside_tile(QK[0], QK[1], m_up)
        PA[11, 32:40, :] = beside_tile(QK[2], QK[3], m_dn)
        PA[12, 32:40, :] = zero8

        @pl.loop(2, 12)
        def _(i):
            PB[i] = relax(PA, i, 40)

        @pl.loop(3, 11)
        def _(i):
            out[i - 3] = relax(PB, i, 32)

        sub, lane = iota((8, 128), 0), iota((8, 128), 1)
        tz = 2 * sub + lane // 64
        ty = (lane % 64) // 8
        tc = (lane % 8) // 2
        odd = lane % 2 == 1

        for copy in halo + gather1 + gather2 + fix_halo + gather3:
            copy.wait_send()
        table = [jnp.where(sub == lax.div(z, 2), M3[k : k + 1, :], 0.0) for k in range(4)]
        for j in sorted(range(nz - 1), key=lambda j: -abs(j - (nz - 2) / 2)):
            from_z = lax.rem(z + nz - 1 - j, nz)
            at = sub == lax.div(from_z, 2)
            gather3[j].wait_recv()
            for k in range(4):
                table[k] = table[k] + jnp.where(at, G3[j, k : k + 1, :], 0.0)
        totals, outs, link_dn, link_cr = table

        def ahead(value, by):
            return pltpu.roll(value, (-by) % 128, 1)

        def shift_rows(value, by):
            return pltpu.roll(value, by % 8, 0)

        def next_parts(value):
            v63 = ahead(value, 63)
            return ahead(value, 1), v63, shift_rows(v63, -1), shift_rows(ahead(value, 71), half - 1)

        def prev_parts(value):
            v63 = ahead(value, -63)
            return (
                ahead(value, -1), v63, shift_rows(v63, 1), shift_rows(ahead(value, -71), 1 - half)
            )

        last = (ty == ny - 1) & (tz == nz - 1)
        first = (ty == 0) & (tz == 0)
        next_at = (
            ~odd,
            odd & (tz % 2 == 0),
            odd & (tz % 2 == 1) & (tz < nz - 1),
            odd & (tz == nz - 1) & ~last,
        )
        prev_at = (
            odd,
            ~odd & (tz % 2 == 1),
            ~odd & (tz % 2 == 0) & (tz > 0),
            ~odd & (tz == 0) & ~first,
        )
        link_up = jnp.zeros((8, 128), F32)
        held = (tz < nz) & (ty < ny) & (tc < n_cross)
        for at, part in zip(prev_at, prev_parts(link_dn)):
            link_up = jnp.where(at & held, part, link_up)
        link_bk = jnp.where((tc > 0) & held, ahead(link_cr, -2), 0.0)
        link_cr = jnp.where(tc < n_cross - 1, link_cr, 0.0)
        next_w = [jnp.where(at, link_dn, 0.0) for at in next_at]
        prev_w = [jnp.where(at, link_up, 0.0) for at in prev_at]

        def operate(value):
            image = outs * value - link_cr * ahead(value, 2) - link_bk * ahead(value, -2)
            for weight, part in zip(next_w, next_parts(value)):
                image = image - weight * part
            for weight, part in zip(prev_w, prev_parts(value)):
                image = image - weight * part
            return image

        def iterate(step, carry):
            answer, resid, search, image, over_norm, over_alpha = carry
            shown = operate(resid)
            norm = total_of(resid * resid)
            weight = total_of(resid * shown)
            beta = norm * over_norm
            alpha = norm / (weight - beta * (norm * over_alpha))
            search = resid + beta * search
            image = shown + beta * image
            answer = answer + alpha * search
            resid = resid - alpha * image
            return answer, resid, search, image, 1.0 / norm, 1.0 / alpha

        none, nil = jnp.zeros((8, 128), F32), jnp.zeros((1, 1), F32)
        start = (none, totals, none, none, nil, nil)
        answer = lax.fori_loop(0, COARSE_ITERS, iterate, start)[0]

        def brick(dd, cc):
            core_b, chip_b = lax.rem(dd, 2), lax.div(dd, 2)
            z_b, y_b = lax.rem(chip_b, nz), lax.div(chip_b, nz)
            at_lane = lax.rem(z_b, 2) * 64 + y_b * 8 + cc * 2 + core_b
            return total_of(jnp.where((sub == lax.div(z_b, 2)) & (lane == at_lane), answer, 0.0))

        mine = brick(d, c)
        near_by = [brick(dd, cc) - mine for dd, cc in near]
        at_corner = [brick(dd, cc) - mine for dd, cc in corners]
        first_half = iota((32, 256), 0) < 16

        @pl.loop(0, 8)
        def _(x):
            out[x, 8:24, :] = out[x, 8:24, :] + mine * GA[x, 8:24, :]
            low, high = out[x, 0:8, :], out[x, 24:32, :]
            out[x, 0:8, :] = low + (mine * GA[x, 0:8, :] + near_by[2] * GS[x, 0:8, :])
            out[x, 24:32, :] = high + (mine * GA[x, 24:32, :] + near_by[3] * GS[x, 8:16, :])

        for k, x in enumerate((0, 1, 6, 7)):
            out[x] = out[x] + near_by[k // 2] * GD[k]
        for k, x in enumerate((0, 7)):
            out[x] = out[x] + jnp.where(first_half, at_corner[2 * k], at_corner[2 * k + 1]) * GC[k]


    return kernel


def solution(mesh):
    n_down, n_cross = mesh.shape["down"], mesh.shape["cross"]
    nz = CHIPS_Z
    ny = n_down // (2 * nz)
    n1 = 2 * n_cross
    big = pltpu.VMEM((14, 40, 256), F32)
    two = pltpu.VMEM((2, 14, 40, 256), F32)
    coarse = pltpu.VMEM((6, 32, 256), F32)
    coarse2 = pltpu.VMEM((2, 6, 32, 256), F32)
    dma = pltpu.SemaphoreType.DMA
    msg = pltpu.VMEM((4, 128), F32)

    def body(right_side, kappa, band_mask, tile_route):
        return pl.pallas_call(
            make_kernel(n_down, n_cross, nz),
            out_shape=pltpu.VMEM(right_side.shape, F32),
            in_specs=[pl.BlockSpec(memory_space=pl.ANY)] * 3
            + [pl.BlockSpec(memory_space=pltpu.SMEM)],
            out_specs=pl.BlockSpec(memory_space=pltpu.VMEM),
            scratch_shapes=[
                big, big, pltpu.VMEM((8, 32, 256), jnp.int32), big, big, big, big, big,
                big, two, two,
                pltpu.VMEM((8, 32, 256), F32),
                pltpu.VMEM((4, 32, 256), F32), coarse, coarse, coarse, coarse2, coarse2,
                coarse, coarse,
                pltpu.VMEM((2, 8, 8, 256), F32), pltpu.VMEM((2, 8, 8, 256), F32),
                pltpu.VMEM((4, 2, 8, 256), F32),
                pltpu.VMEM((2, 8, 8, 256), F32), pltpu.VMEM((4, 8, 256), F32),
                big, big, pltpu.VMEM((14, 24, 256), F32),
                pltpu.VMEM((8, 32, 256), F32), pltpu.VMEM((8, 16, 256), F32),
                pltpu.VMEM((4, 32, 256), F32), pltpu.VMEM((2, 32, 256), F32),
                msg, pltpu.VMEM((n1 - 1, 4, 128), F32),
                msg, pltpu.VMEM((ny - 1, 4, 128), F32),
                msg, pltpu.VMEM((nz - 1, 4, 128), F32),
                dma((3,)), dma((10,)), dma((10,)), dma((8,)), dma((8,)),
                dma((n1 - 1,)), dma((n1 - 1,)), dma((ny - 1,)), dma((ny - 1,)),
                dma((nz - 1,)), dma((nz - 1,)), pltpu.SemaphoreType.REGULAR((3,)),
            ],
            compiler_params=pltpu.CompilerParams(collective_id=0, has_side_effects=True),
            name="cycle",
        )(right_side, kappa, band_mask, tile_route)

    return jax.shard_map(
        body,
        mesh=mesh,
        in_specs=(
            P("down", "cross", None),
            P("down", "cross", None),
            P("down", "cross", None),
            P("down", "cross"),
        ),
        out_specs=P("down", "cross", None),
        check_vma=False,
    )
```
